32 devices in a mesh: phase: 2 (over x), expert: 4 (over y, core), tensor: 4 (over z).
Axes of the slice: x: 2, y: 2, z: 4, core: 2. Of those that a mesh axis runs over, the one named last changes fastest.
Arguments:
- forward_routes: int32 [2, 256, 6], P('phase', 'expert'), may hold values from 0 to 11, all different within a row; in each aligned block of 64 rows (0 to 63, 64 to 127, ..., all dimensions but the last counted through in order) at most 43 rows name the same one
- forward_gates: float32 [2, 256, 6], P('phase', 'expert'), may hold values from 0.05 to 1
- hidden_rows: bfloat16 [2, 12, 4, 43, 1024], P('phase', 'expert', None, None, 'tensor'), may hold values from -6 to 6
- down_weight: bfloat16 [2, 12, 1024, 2560], P('phase', 'expert', 'tensor'), may hold values from -0.1875 to 0.1875
- shared_hidden: bfloat16 [2, 256, 1536], P('phase', 'expert', 'tensor'), may hold values from -6 to 6
- shared_weight: bfloat16 [2, 1536, 2560], P('phase', 'tensor', 'expert'), may hold values from -0.15625 to 0.15625
- backward_routes: int32 [2, 256, 6], P('phase', 'expert'), may hold values from 0 to 11, all different within a row; in each aligned block of 64 rows (0 to 63, 64 to 127, ..., all dimensions but the last counted through in order) at most 43 rows name the same one
- backward_gates: float32 [2, 256, 6], P('phase', 'expert'), may hold values from 0.05 to 1
- cotangent: bfloat16 [2, 256, 2560], P('phase', 'expert', 'tensor'), may hold values from -6 to 6
Outputs:
- forward_next: bfloat16 [2, 256, 2560], P('phase', 'expert', 'tensor')
- hidden_grad: bfloat16 [2, 12, 4, 43, 1024], P('phase', 'expert', None, None, 'tensor')
- shared_grad: bfloat16 [2, 256, 1536], P('phase', 'expert', 'tensor')
The draws below stay inside these ranges and needn't reach their ends.
Inputs may be any that keep to these rules, and one draw needn't show every extreme that they name: `forward_routes`: each token names 6 different experts. The tokens of one token group (the 64 rows of one device) name any one expert 43 times at most, and some group reaches that. `backward_routes`: as for forward_routes.
All inputs are finite; a program needn't handle non-finite values.
Results may differ from the reference program's by a relative error of at most 0.0049.
Values may be sent and summed in bfloat16 or wider, within the bound.
A program may use at most 64 MiB of HBM per device.

```python
import math
import jax
import jax.numpy as jnp
import numpy as np
from jax import lax

D = 2560
HID = 1024
HS = 1536
TOPK = 6
TOK_DEV = 64
SECTIONS = 2
GROUPS = 4
HPARTS = 4
EXPERTS = 12
TOKENS = 256
MOST = 43


def shard_levels(own_key, extent, split, low, top_value):
    def one(dim, blocks):
        heights = jax.random.uniform(jax.random.fold_in(jax.random.fold_in(own_key, 6), dim), (blocks,), jnp.float32, low / len(split), top_value / len(split))
        return jnp.repeat(jnp.exp(heights), extent[dim] // blocks).reshape((-1,) + (1,) * (len(extent) - dim - 1))

    loudness = one(*split[0])
    for cut in split[1:]:
        loudness = loudness * one(*cut)
    return loudness


def deal_out(rng, own, number, rows, number_of, top, limit, skew):
    ranking = jax.random.permutation(rng, number_of)
    crowded, ordinary = shares(number_of, rows * top, limit, skew, True), shares(number_of, rows * top, limit, skew, False)
    places = jnp.arange(number_of)

    def named(tallies, offset_by):
        used = int((tallies > 0).sum())
        fixed = max(1, used // 4)
        moved = fixed + (places - fixed + offset_by * (used - fixed)) % max(1, number_of - fixed)
        return jnp.zeros((number_of,), jnp.int32).at[ranking[jnp.where(places < fixed, places, moved)]].set(jnp.asarray(tallies, jnp.int32))

    tallies = jnp.where(number % 4 == 0, named(crowded, number // 4), named(ordinary, number - number // 4 - 1))
    mixed = jax.random.permutation(jax.random.fold_in(own, 3), number_of)
    giver, taker = mixed[0:number_of // 2 * 2:2], mixed[1:number_of // 2 * 2:2]
    room = jnp.minimum(tallies[giver] - 1, limit - tallies[taker]) // 2
    room = jnp.where((giver == ranking[0]) | (taker == ranking[0]) | (tallies[taker] == 0), 0, jnp.maximum(room, 0))
    moved = jax.random.randint(jax.random.fold_in(own, 4), (number_of // 2,), 0, 1 << 20) % (room + 1)
    tallies = tallies.at[giver].add(-moved).at[taker].add(moved)
    labels = jnp.searchsorted(jnp.cumsum(tallies), jnp.arange(rows * top), side="right").astype(jnp.int32)
    listing = labels.reshape(top, rows).T
    listing = listing[jax.random.permutation(jax.random.fold_in(own, 1), rows)]
    offset_by = jax.random.randint(jax.random.fold_in(own, 2), (rows, 1), 0, top)
    return jnp.take_along_axis(listing, (jnp.arange(top)[None, :] + offset_by) % top, axis=1)


def shares(amount, total, bound, lean, full):
    loads = [(1 << 20) // math.isqrt(rank ** lean) + 1 for rank in range(1, amount + 1)]
    largest = bound if full else min(bound, max(-(-total // amount), total * loads[0] // sum(loads)))
    least = 1 if total - largest >= amount - 1 else 0
    counts, spare = [largest] + [least] * (amount - 1), total - largest - least * (amount - 1)
    while spare > 0:
        free = [i for i in range(1, amount) if counts[i] < largest] or [i for i in range(1, amount) if counts[i] < bound]
        whole, left = sum([loads[i] for i in free]), spare
        for i in free:
            extra = min(bound - counts[i], max(1, left * loads[i] // whole), spare)
            counts[i] = counts[i] + extra
            spare = spare - extra
    return np.array(counts)


def normal_values(own_key, shape, width, limit, split=(), kind=jnp.bfloat16):
    level = shard_levels(own_key, shape, split, -0.22, 0.18) if split else 1.0
    array = jax.random.normal(own_key, shape, jnp.float32) * width * level
    return jnp.minimum(jnp.maximum(array, -limit), limit).astype(kind)


def setup_inputs(seed: int = 0) -> dict:
    key_list = jax.random.split(jax.random.key(seed), 10)
    forward_routes_keys = jax.random.split(jax.random.fold_in(key_list[0], 1), SECTIONS * TOKENS // TOK_DEV)
    forward_routes_turns = jax.random.permutation(jax.random.fold_in(key_list[0], 3), SECTIONS * TOKENS // TOK_DEV)
    forward_routes = jax.vmap(lambda own, number: deal_out(jax.random.fold_in(key_list[0], 2), own, number, TOK_DEV, EXPERTS, TOPK, MOST, 2))(forward_routes_keys, forward_routes_turns).reshape((SECTIONS, TOKENS, TOPK))
    forward_gates = jnp.clip(jnp.exp(math.log(1.0) - 2.9957323 * jax.random.uniform(key_list[1], (SECTIONS, TOKENS, TOPK), jnp.float32) ** shard_levels(key_list[1], (SECTIONS, TOKENS, TOPK), ((0, 2), (1, 4)), -0.2, 0.2)), 0.05, 1.0)
    hidden_rows = normal_values(key_list[2], (SECTIONS, EXPERTS, GROUPS, MOST, HID), 1.0, 6.0, ((0, 2), (1, 4), (4, 4)))
    down_weight = normal_values(key_list[3], (SECTIONS, EXPERTS, HID, D), HID ** -0.5, 0.1875, ((0, 2), (1, 4), (2, 4)))
    shared_hidden = normal_values(key_list[4], (SECTIONS, TOKENS, HS), 1.0, 6.0, ((0, 2), (1, 4), (2, 4)))
    shared_weight = normal_values(key_list[5], (SECTIONS, HS, D), HS ** -0.5, 0.15625, ((0, 2), (1, 4), (2, 4)))
    backward_routes_keys = jax.random.split(jax.random.fold_in(key_list[6], 1), SECTIONS * TOKENS // TOK_DEV)
    backward_routes_turns = jax.random.permutation(jax.random.fold_in(key_list[6], 3), SECTIONS * TOKENS // TOK_DEV)
    backward_routes = jax.vmap(lambda own, number: deal_out(jax.random.fold_in(key_list[6], 2), own, number, TOK_DEV, EXPERTS, TOPK, MOST, 2))(backward_routes_keys, backward_routes_turns).reshape((SECTIONS, TOKENS, TOPK))
    backward_gates = jnp.clip(jnp.exp(math.log(1.0) - 2.9957323 * jax.random.uniform(key_list[7], (SECTIONS, TOKENS, TOPK), jnp.float32) ** shard_levels(key_list[7], (SECTIONS, TOKENS, TOPK), ((0, 2), (1, 4)), -0.2, 0.2)), 0.05, 1.0)
    cotangent = normal_values(key_list[8], (SECTIONS, TOKENS, D), 1.0, 6.0, ((0, 2), (1, 4), (2, 4)))
    return {"forward_routes": forward_routes, "forward_gates": forward_gates, "hidden_rows": hidden_rows, "down_weight": down_weight, "shared_hidden": shared_hidden, "shared_weight": shared_weight, "backward_routes": backward_routes, "backward_gates": backward_gates, "cotangent": cotangent}


def slot_numbers(routes, experts):
    numbers = jnp.arange(experts, dtype=jnp.int32)
    onehot = (routes[:, :, None] == numbers[None, None, :]).astype(jnp.int32)
    per_token = jnp.sum(onehot, axis=1)
    before = jnp.cumsum(per_token, axis=0) - per_token
    return jnp.sum(onehot * before[:, None, :], axis=2)


def block_slots(block_routes):
    return slot_numbers(block_routes, EXPERTS)


def positions(routes):
    blocks = routes.reshape(GROUPS, TOK_DEV, TOPK)
    slot_index = jax.vmap(block_slots)(blocks).reshape(TOKENS, TOPK)
    block_index = (jnp.arange(TOKENS, dtype=jnp.int32) // TOK_DEV)[:, None]
    return ((routes * GROUPS + block_index) * MOST + slot_index).reshape(-1)


def forward_rows(operands):
    hidden_block, matrix = operands
    left_side = hidden_block.reshape(GROUPS * MOST, HPARTS, HID // HPARTS).astype(jnp.float32)
    right_side = matrix.reshape(HPARTS, HID // HPARTS, D).astype(jnp.float32)
    pieces = jnp.einsum("rqh,qhd->rqd", left_side, right_side, precision=lax.Precision.HIGHEST).astype(jnp.bfloat16)
    pieces = lax.optimization_barrier(pieces)
    return jnp.sum(pieces.astype(jnp.float32), axis=1)


def backward_rows(operands):
    sent_block, matrix = operands
    return jnp.dot(sent_block, matrix.T, preferred_element_type=jnp.float32).astype(jnp.bfloat16)


def reference(forward_routes, forward_gates, hidden_rows, down_weight, shared_hidden, shared_weight, backward_routes, backward_gates, cotangent):
    layers = []
    hidden_grads = []
    shared_grads = []
    for section in range(SECTIONS):
        fore_positions = positions(forward_routes[section])
        summed = lax.map(forward_rows, (hidden_rows[section], down_weight[section])).reshape(-1, D)
        picked = summed[fore_positions].reshape(TOKENS, TOPK, D)
        routed = jnp.sum(picked * forward_gates[section][:, :, None], axis=1)
        shared_out = jnp.dot(shared_hidden[section], shared_weight[section], preferred_element_type=jnp.float32)
        layers.append((routed + shared_out).astype(jnp.bfloat16))
        back_positions = positions(backward_routes[section])
        scaled = (backward_gates[section][:, :, None] * cotangent[section][:, None, :].astype(jnp.float32)).astype(jnp.bfloat16)
        outgoing = jnp.zeros((EXPERTS * GROUPS * MOST, D), jnp.bfloat16).at[back_positions].set(scaled.reshape(-1, D))
        expert_grads = lax.map(backward_rows, (outgoing.reshape(EXPERTS, GROUPS * MOST, D), down_weight[section]))
        hidden_grads.append(expert_grads.reshape(EXPERTS, GROUPS, MOST, HID))
        shared_grads.append(jnp.dot(cotangent[section], shared_weight[section].T, preferred_element_type=jnp.float32).astype(jnp.bfloat16))
    forward_next = jnp.roll(jnp.stack(layers), 1, axis=0)
    return forward_next, jnp.stack(hidden_grads), jnp.stack(shared_grads)
```

```python
import functools

import jax
import jax.numpy as jnp
from jax import lax
from jax.experimental import pallas as pl
from jax.experimental.pallas import tpu as pltpu
from jax.sharding import PartitionSpec as P

MESH = pl.DeviceIdType.MESH
LANES = 128
F32 = jnp.float32
BF16 = jnp.bfloat16


def fused_kernel(
    sizes,
    fr_ref, fg_ref, br_ref, bg_ref,
    hid_hbm, w_hbm, sh_hbm, sw_hbm, cot_hbm,
    next_ref, hgrad_ref, sgrad_ref,
    hid, w, sw, sh, cot, pack, hc, acc, keep,
    s1_out, s1_in, s2_out, s2_in, s3_out, s3_in, s4_out,
    back, sg_part, sg_out, sg_in,
    send_sem, recv_sem, load_sem,
):
    (phases, ne, nt) = sizes
    ph, e, z = lax.axis_index("phase"), lax.axis_index("expert"), lax.axis_index("tensor")
    tok, top = fr_ref.shape
    here, cap, hq = hid.shape[0] // ne, hid.shape[1], hid.shape[2]
    dt = cot.shape[3]
    hs = sw.shape[0]
    experts = here * ne
    core = lax.rem(e, 2)
    sib = e + 1 - 2 * core
    far = lax.rem(e + 2, ne)
    far_sib = lax.rem(sib + 2, ne)
    others_e = [lax.rem(e + r, ne) for r in range(1, ne)]
    others_t = [lax.rem(z + d, nt) for d in range(1, nt)]

    loads = [
        pltpu.make_async_copy(hid_hbm, hid, load_sem.at[0]),
        pltpu.make_async_copy(w_hbm, w, load_sem.at[1]),
        pltpu.make_async_copy(sw_hbm, sw, load_sem.at[2]),
        pltpu.make_async_copy(sh_hbm, sh.at[e], load_sem.at[3]),
        pltpu.make_async_copy(cot_hbm, cot.at[z, e], load_sem.at[4]),
    ]
    for i in (4, 3, 0, 1, 2):
        loads[i].start()

    barrier = pltpu.get_barrier_semaphore()
    partners = [{"expert": o} for o in others_e] + [{"tensor": o} for o in others_t]
    ahead, behind = lax.rem(ph + 1, phases), lax.rem(ph + phases - 1, phases)
    partners.append({"phase": ahead})
    if phases > 2:
        partners.append({"phase": behind})
    for partner in partners:
        pl.semaphore_signal(barrier, inc=1, device_id=partner, device_id_type=MESH)

    lane = lax.broadcasted_iota(jnp.int32, (tok, LANES), 1)
    hot = jnp.zeros((tok, LANES), F32)
    gate = jnp.zeros((tok, LANES), F32)
    for direction, (routes, gates) in enumerate(((fr_ref, fg_ref), (br_ref, bg_ref))):
        base = 2 * direction * experts
        for k in range(top):
            named = routes[:, k:k + 1] + base
            hot = jnp.where(named == lane, 1.0, hot)
            gate = jnp.where(named + experts == lane, gates[:, k:k + 1], gate)
    row = lax.broadcasted_iota(jnp.int32, (tok, tok), 0)
    column = lax.broadcasted_iota(jnp.int32, (tok, tok), 1)
    earlier = jnp.where(row > column, 1.0, 0.0).astype(BF16)
    slots = jnp.dot(earlier, hot.astype(BF16), preferred_element_type=F32)
    is_slot = (lane < experts) | ((lane >= 2 * experts) & (lane < 3 * experts))
    pack[e] = jnp.where(is_slot, jnp.where(hot > 0.5, slots, -1.0), gate)

    copies = []

    def send(src, dst, to):
        i = len(copies)
        copy = pltpu.make_async_remote_copy(
            src_ref=src, dst_ref=dst, send_sem=send_sem.at[i], recv_sem=recv_sem.at[i],
            device_id=to, device_id_type=MESH,
        )
        copy.start()
        copies.append(copy)
        return copy

    pl.semaphore_wait(barrier, len(partners))
    pack_copies = [send(pack.at[e], pack.at[e], {"expert": o}) for o in others_e]
    loads[4].wait()
    mine = cot.at[z, e]
    z_copies = [send(mine, mine, {"tensor": o}) for o in others_t]
    y_copies = [send(mine, mine, {"expert": far})]
    sib_copies = [send(mine, mine, {"expert": sib})]
    loads[3].wait()
    sh_copies = [send(sh.at[e], sh.at[e], {"expert": o}) for o in others_e]

    order = (far_sib, sib, far, e)
    slot_at = lax.broadcasted_iota(jnp.int32, (tok, cap), 1).astype(F32)

    def pick(table, at):
        return jnp.sum(jnp.where(lane == at, table, 0.0), axis=1, keepdims=True)

    for copy in pack_copies:
        copy.wait_recv()
    loads[0].wait()
    for n, b in enumerate(order):
        table = pack[b]
        for i in range(here):
            x = e * here + i
            place = jnp.where(pick(table, x) == slot_at, 1.0, 0.0).astype(BF16)
            rows = jnp.dot(place, hid[i * ne + b], preferred_element_type=F32)
            hc[n * tok:(n + 1) * tok, i * hq:(i + 1) * hq] = (
                rows * pick(table, experts + x)
            ).astype(BF16)

    def relay(d):
        z_copies[d - 1].wait_recv()
        piece = cot.at[lax.rem(z + nt - d, nt), e]
        y_copies.append(send(piece, piece, {"expert": far}))
        sib_copies.append(send(piece, piece, {"expert": sib}))

    loads[1].wait()
    loads[2].wait()
    for copy in sh_copies:
        copy.wait_recv()
    s1, s2, s3 = [], [], []
    for s in range(nt):
        f = lax.rem(z + 1 + s, nt)
        cols = pl.ds(pl.multiple_of(f * dt, LANES), dt)
        acc[...] = jnp.dot(hc[...], w[:, cols], preferred_element_type=F32)

        @pl.when(f == e)
        def _():
            shared = jnp.concatenate([sh[b] for b in order], axis=0)
            acc[...] += jnp.dot(shared, sw[...], preferred_element_type=F32)

        for g in range(2):
            s1_out[s, g] = acc[g * tok:(g + 1) * tok, :].astype(BF16)
        s1.append(send(s1_out.at[s], s1_in.at[s], {"expert": sib}))
        for g in range(2):
            keep[s, g] = acc[(2 + g) * tok:(3 + g) * tok, :]
        if s >= 1:
            relay(s)
    for s in range(nt):
        s1[s].wait_recv()
        s2_out[s] = (keep[s, 0] + s1_in[s, 0].astype(F32)).astype(BF16)
        s2.append(send(s2_out.at[s], s2_in.at[s], {"expert": far}))
        keep[s, 1] = keep[s, 1] + s1_in[s, 1].astype(F32)

    far_copies = []

    def hand_over(d):
        y_copies[d].wait_recv()
        piece = cot.at[lax.rem(z + nt - d, nt), far]
        far_copies.append(send(piece, piece, {"expert": sib}))

    def back_part(d):
        f = lax.rem(z + nt - d, nt)
        sib_copies[d].wait_recv()
        far_copies[d].wait_recv()
        cols = pl.ds(pl.multiple_of(f * dt, LANES), dt)
        rows = cot[f].reshape(ne * tok, dt)
        part = lax.dot_general(
            rows, w[:, cols], (((1,), (1,)), ((), ())), preferred_element_type=F32
        )
        if d == 0:
            back[...] = part
        else:
            back[...] += part

    def reduce_z(s):
        s2[s].wait_recv()
        total = keep[s, 1] + s2_in[s].astype(F32)
        if s < nt - 1:
            s3_out[s] = total.astype(BF16)
            s3.append(send(s3_out.at[s], s3_in.at[s], {"tensor": others_t[s]}))
        else:
            keep[s, 1] = total

    for d in range(nt):
        hand_over(d)
        reduce_z(d)
    for d in range(nt):
        back_part(d)

    sg_part[...] = lax.dot_general(
        cot[e].reshape(ne * tok, dt), sw[...], (((1,), (1,)), ((), ())),
        preferred_element_type=F32,
    ).reshape(ne, tok, hs)
    sg = []
    for r, o in enumerate(others_e):
        sg_out[r] = sg_part[o].astype(BF16)
        sg.append(send(sg_out.at[r], sg_in.at[r], {"expert": o}))

    total = keep[nt - 1, 1]
    for s in range(nt - 1):
        s3[s].wait_recv()
        total = total + s3_in[s].astype(F32)
    s4_out[...] = total.astype(BF16)
    s4 = send(s4_out, next_ref, {"phase": ahead})

    for b in range(ne):
        table = pack[b]
        for i in range(here):
            x = 2 * experts + e * here + i
            place = jnp.where(pick(table, x) == slot_at, 1.0, 0.0).astype(BF16)
            rows = back[b * tok:(b + 1) * tok, i * hq:(i + 1) * hq]
            rows = (rows * pick(table, experts + x)).astype(BF16)
            hgrad_ref[i * ne + b] = lax.dot_general(
                place, rows, (((0,), (0,)), ((), ())), preferred_element_type=F32
            ).astype(BF16)

    shared_total = sg_part[e]
    for copy in sg:
        copy.wait_recv()
    for r in range(ne - 1):
        shared_total = shared_total + sg_in[r].astype(F32)
    sgrad_ref[...] = shared_total.astype(BF16)
    s4.wait_recv()
    for copy in copies:
        copy.wait_send()


def fused(sizes, fr, fg, hidden, weight, shared, sweight, br, bg, cot):
    phases, ne, nt = sizes
    here, groups, cap, hq = hidden.shape[1:]
    tok = fr.shape[1]
    features = weight.shape[3]
    dt = cot.shape[2]
    hs = shared.shape[2]
    vmem = pl.BlockSpec(memory_space=pltpu.VMEM)
    anywhere = pl.BlockSpec(memory_space=pl.ANY)
    copies = 3 * (ne - 1) + 2 * (nt - 1) + 6 * nt - nt + 1
    rows = ne * tok
    handed, hgrad, sgrad = pl.pallas_call(
        functools.partial(fused_kernel, sizes),
        out_shape=(
            jax.ShapeDtypeStruct((tok, dt), BF16),
            jax.ShapeDtypeStruct((here * groups, cap, hq), BF16),
            jax.ShapeDtypeStruct((tok, hs), BF16),
        ),
        in_specs=[vmem] * 4 + [anywhere] * 5,
        out_specs=(vmem, vmem, vmem),
        scratch_shapes=[
            pltpu.VMEM((here * groups, cap, hq), BF16),
            pltpu.VMEM((here * hq, features), BF16),
            pltpu.VMEM((hs, dt), BF16),
            pltpu.VMEM((ne, tok, hs), BF16),
            pltpu.VMEM((nt, ne, tok, dt), BF16),
            pltpu.VMEM((ne, tok, LANES), F32),
            pltpu.VMEM((rows, here * hq), BF16),
            pltpu.VMEM((rows, dt), F32),
            pltpu.VMEM((nt, 2, tok, dt), F32),
            pltpu.VMEM((nt, 2, tok, dt), BF16),
            pltpu.VMEM((nt, 2, tok, dt), BF16),
            pltpu.VMEM((nt, tok, dt), BF16),
            pltpu.VMEM((nt, tok, dt), BF16),
            pltpu.VMEM((nt - 1, tok, dt), BF16),
            pltpu.VMEM((nt - 1, tok, dt), BF16),
            pltpu.VMEM((tok, dt), BF16),
            pltpu.VMEM((rows, here * hq), F32),
            pltpu.VMEM((ne, tok, hs), F32),
            pltpu.VMEM((ne - 1, tok, hs), BF16),
            pltpu.VMEM((ne - 1, tok, hs), BF16),
            pltpu.SemaphoreType.DMA((copies,)),
            pltpu.SemaphoreType.DMA((copies,)),
            pltpu.SemaphoreType.DMA((5,)),
        ],
        compiler_params=pltpu.CompilerParams(
            collective_id=0, has_side_effects=True, vmem_limit_bytes=48 * 1024 * 1024
        ),
    )(
        fr[0], fg[0], br[0], bg[0],
        hidden.reshape(here * groups, cap, hq),
        weight.reshape(here * hq, features),
        shared[0], sweight[0], cot[0],
    )
    return handed[None], hgrad.reshape(hidden.shape), sgrad[None]


def shifted(value, axis, steps):
    count = lax.axis_size(axis)
    pairs = [(source, (source + steps) % count) for source in range(count)]
    return lax.ppermute(value, axis, pairs)


def slot_numbers(routes, experts):
    numbers = jnp.arange(experts, dtype=jnp.int32)
    onehot = (routes[:, :, None] == numbers[None, None, :]).astype(jnp.int32)
    per_token = jnp.sum(onehot, axis=1)
    before = jnp.cumsum(per_token, axis=0) - per_token
    return jnp.sum(onehot * before[:, None, :], axis=2)


def row_positions(routes, experts_here, groups, capacity):
    slot_index = slot_numbers(routes, experts_here * groups)
    holder = routes // experts_here
    within = routes - holder * experts_here
    return ((within * groups + holder) * capacity + slot_index).reshape(-1)


def place_rows(gates, values, positions, total_rows):
    scaled = (gates[:, :, None] * values[:, None, :].astype(jnp.float32)).astype(jnp.bfloat16)
    outgoing = jnp.zeros((total_rows, values.shape[1]), jnp.bfloat16)
    return outgoing.at[positions].set(scaled.reshape(-1, values.shape[1]))


def unfused(
    forward_routes,
    forward_gates,
    hidden_rows,
    down_weight,
    shared_hidden,
    shared_weight,
    backward_routes,
    backward_gates,
    cotangent,
):
    experts_here = down_weight.shape[1]
    features = down_weight.shape[3]
    capacity = hidden_rows.shape[3]
    groups = lax.axis_size("expert")
    token_count = forward_routes.shape[1]
    top_count = forward_routes.shape[2]
    hidden = hidden_rows[0]
    weight = down_weight[0]
    local_shared = shared_hidden[0]
    shared_piece = shared_weight[0]
    shared_part = jnp.dot(
        local_shared,
        lax.all_gather(shared_piece, "expert", axis=1, tiled=True),
        preferred_element_type=jnp.float32,
    )
    fore_positions = row_positions(forward_routes[0], experts_here, groups, capacity)
    fore_gates = forward_gates[0]
    partial_value = jnp.einsum(
        "egmh,ehd->egmd", hidden, weight, preferred_element_type=jnp.float32
    ).astype(jnp.bfloat16)
    arrived = lax.all_to_all(partial_value, "expert", split_axis=1, concat_axis=1, tiled=True)
    picked = arrived.reshape(-1, features)[fore_positions].reshape(token_count, top_count, features)
    summand = shared_part + jnp.sum(picked.astype(jnp.float32) * fore_gates[:, :, None], axis=1)
    summed = lax.psum_scatter(summand, "tensor", scatter_dimension=1, tiled=True)
    layer_out = summed.astype(jnp.bfloat16)
    handed = shifted(layer_out, "phase", 1)
    cotangent_whole = lax.all_gather(cotangent[0], "tensor", axis=1, tiled=True)
    back_positions = row_positions(backward_routes[0], experts_here, groups, capacity)
    total_rows = experts_here * groups * capacity
    outgoing = place_rows(backward_gates[0], cotangent_whole, back_positions, total_rows)
    received = lax.all_to_all(
        outgoing.reshape(experts_here, groups, capacity, features),
        "expert",
        split_axis=1,
        concat_axis=1,
        tiled=True,
    )
    hidden_back = jnp.einsum(
        "egmd,ehd->egmh", received, weight, preferred_element_type=jnp.float32
    ).astype(jnp.bfloat16)
    shared_back = lax.dot_general(
        cotangent_whole,
        lax.all_gather(shared_piece, "expert", axis=1, tiled=True),
        (((1,), (1,)), ((), ())),
        preferred_element_type=jnp.float32,
    )
    return (handed[None], hidden_back[None], shared_back.astype(jnp.bfloat16)[None])


def solution(mesh):
    sizes = tuple(mesh.shape[axis] for axis in ("phase", "expert", "tensor"))

    def on_device(*arrays):
        phases, ne, nt = sizes
        hidden, weight, cot = arrays[2], arrays[3], arrays[8]
        two_chips = ne == 4 and ne == nt and phases > 1
        fits = 4 * ne * weight.shape[1] <= LANES and cot.shape[2] % LANES == 0
        if two_chips and fits:
            return fused(sizes, *arrays)
        return unfused(*arrays)

    return jax.shard_map(
        on_device,
        mesh=mesh,
        in_specs=(
            P("phase", "expert", None),
            P("phase", "expert", None),
            P("phase", "expert", None, None, "tensor"),
            P("phase", "expert", "tensor", None),
            P("phase", "expert", "tensor"),
            P("phase", "tensor", "expert"),
            P("phase", "expert", None),
            P("phase", "expert", None),
            P("phase", "expert", "tensor"),
        ),
        out_specs=(
            P("phase", "expert", "tensor"),
            P("phase", "expert", None, None, "tensor"),
            P("phase", "expert", "tensor"),
        ),
        check_vma=False,
    )
```

```python
import functools

import jax
import jax.numpy as jnp
from jax import lax
from jax.experimental import pallas as pl
from jax.experimental.pallas import tpu as pltpu
from jax.sharding import PartitionSpec as P

MESH = pl.DeviceIdType.MESH
LANES = 128
F32 = jnp.float32
BF16 = jnp.bfloat16


def fused_kernel(
    sizes,
    fr_hbm, fg_hbm, br_hbm, bg_hbm,
    hid_hbm, w_hbm, sh_hbm, sw_hbm, cot_hbm,
    next_ref, hgrad_ref, sgrad_ref,
    fr, fg, br, bg,
    hid, w, sw, sh, cot, pack, hc, acc, keep,
    s1_out, s1_in, s2_out, s2_in, s3_out, s3_in,
    back, sg_part, sg_out, sg_in, sg_out2, sg_in2,
    send_sem, recv_sem, load_sem,
):
    phases, ne, nt = sizes
    ph, e, z = lax.axis_index("phase"), lax.axis_index("expert"), lax.axis_index("tensor")
    top, _, tok = fr.shape
    here, cap, _, hq = hid.shape
    dt = cot.shape[3]
    hs = sw.shape[0]
    experts = here * ne
    slots_all = cap * ne
    core = lax.rem(e, 2)
    sib = e + 1 - 2 * core
    far = lax.rem(e + 2, ne)
    far_sib = lax.rem(sib + 2, ne)
    others_t = [lax.rem(z + d, nt) for d in range(1, nt)]
    ahead, behind = lax.rem(ph + 1, phases), lax.rem(ph + phases - 1, phases)

    pairs = (
        (fr_hbm, fr), (fg_hbm, fg), (br_hbm, br), (bg_hbm, bg),
        (cot_hbm, cot.at[z, e]), (sh_hbm, sh.at[e]), (hid_hbm, hid), (w_hbm, w), (sw_hbm, sw),
    )
    loads = [pltpu.make_async_copy(a, b, load_sem.at[i]) for i, (a, b) in enumerate(pairs)]
    for load in loads:
        load.start()

    barrier = pltpu.get_barrier_semaphore()
    partners = [{"expert": sib}, {"expert": far}] + [{"tensor": o} for o in others_t]
    for step in range(nt):
        partners.append({"phase": ahead, "tensor": lax.rem(z + step, nt)})
        if phases > 2:
            partners.append({"phase": behind, "tensor": lax.rem(z + step, nt)})
    for partner in partners:
        pl.semaphore_signal(barrier, inc=1, device_id=partner, device_id_type=MESH)

    for load in loads[:4]:
        load.wait()
    across = 2 * experts
    level = lax.broadcasted_iota(jnp.int32, (across, 2 * tok), 0)
    hot = jnp.zeros((across, 2 * tok), F32)
    gate = jnp.zeros((across, 2 * tok), F32)
    for k in range(top):
        named = jnp.concatenate([fr[k], br[k]], axis=1)
        weigh = jnp.concatenate([fg[k], bg[k]], axis=1)
        hot = jnp.where(named == level, 1.0, hot)
        gate = jnp.where(named + experts == level, weigh, gate)
    first = lax.broadcasted_iota(jnp.int32, (2 * tok, 2 * tok), 0)
    second = lax.broadcasted_iota(jnp.int32, (2 * tok, 2 * tok), 1)
    earlier = (first < second) & ((first < tok) == (second < tok))
    counts = jnp.dot(
        hot.astype(BF16), jnp.where(earlier, 1.0, 0.0).astype(BF16), preferred_element_type=F32
    )
    pack[e] = jnp.where(level < experts, jnp.where(hot > 0.5, counts, -1.0), gate)

    copies = []

    def send(src, dst, to):
        i = len(copies)
        copy = pltpu.make_async_remote_copy(
            src_ref=src, dst_ref=dst, send_sem=send_sem.at[i], recv_sem=recv_sem.at[i],
            device_id=to, device_id_type=MESH,
        )
        copy.start()
        copies.append(copy)
        return copy

    def spread(buffer):
        return [send(buffer.at[e], buffer.at[e], {"expert": o}) for o in (far, sib)]

    def hand_on(buffer, pair):
        pair[0].wait_recv()
        pair.append(send(buffer.at[far], buffer.at[far], {"expert": sib}))

    pl.semaphore_wait(barrier, len(partners))
    pack_copies = spread(pack)
    loads[5].wait()
    sh_copies = spread(sh)
    loads[4].wait()
    mine = cot.at[z, e]
    z_copies = [send(mine, mine, {"tensor": o}) for o in others_t]
    y_copies = [send(mine, mine, {"expert": far})]
    sib_copies = [send(mine, mine, {"expert": sib})]
    hand_on(pack, pack_copies)
    hand_on(sh, sh_copies)

    order = (far_sib, sib, far, e)
    level = lax.broadcasted_iota(jnp.int32, (tok, across), 1)
    entry = lax.broadcasted_iota(jnp.int32, (tok, slots_all), 1).astype(F32)

    def pick(table, at):
        return jnp.sum(jnp.where(level == at, table, 0.0), axis=1, keepdims=True)

    pack_copies[1].wait_recv()
    pack_copies[2].wait_recv()
    loads[6].wait()
    hidden = [hid[i].reshape(slots_all, hq) for i in range(here)]
    for n, b in enumerate(order):
        table = pack[b].T[:tok]
        offset = b.astype(F32)
        for i in range(here):
            x = e * here + i
            place = jnp.where(pick(table, x) * ne + offset == entry, 1.0, 0.0).astype(BF16)
            rows = jnp.dot(place, hidden[i], preferred_element_type=F32)
            hc[n * tok:(n + 1) * tok, i * hq:(i + 1) * hq] = (
                rows * pick(table, experts + x)
            ).astype(BF16)

    def relay(d):
        z_copies[d - 1].wait_recv()
        piece = cot.at[lax.rem(z + nt - d, nt), e]
        y_copies.append(send(piece, piece, {"expert": far}))
        sib_copies.append(send(piece, piece, {"expert": sib}))

    relay(1)
    loads[7].wait()
    loads[8].wait()
    sh_copies[1].wait_recv()
    sh_copies[2].wait_recv()
    s1, s2, s3 = [], [], []
    for s in range(nt):
        f = lax.rem(z + 1 + s, nt)
        cols = pl.ds(pl.multiple_of(f * dt, LANES), dt)
        acc[...] = jnp.dot(hc[...], w[:, cols], preferred_element_type=F32)

        @pl.when(f == e)
        def _():
            shared = jnp.concatenate([sh[b] for b in order], axis=0)
            acc[...] += jnp.dot(shared, sw[...], preferred_element_type=F32)

        for g in range(2):
            s1_out[s, g] = acc[g * tok:(g + 1) * tok, :].astype(BF16)
        s1.append(send(s1_out.at[s], s1_in.at[s], {"expert": sib}))
        for g in range(2):
            keep[s, g] = acc[(2 + g) * tok:(3 + g) * tok, :]
        if 1 <= s < nt - 1:
            relay(s + 1)
    for s in range(nt):
        s1[s].wait_recv()
        s2_out[s] = (keep[s, 0] + s1_in[s, 0].astype(F32)).astype(BF16)
        s2.append(send(s2_out.at[s], s2_in.at[s], {"expert": far}))
        keep[s, 1] = keep[s, 1] + s1_in[s, 1].astype(F32)

    far_copies = []
    for d in range(nt):
        y_copies[d].wait_recv()
        piece = cot.at[lax.rem(z + nt - d, nt), far]
        far_copies.append(send(piece, piece, {"expert": sib}))

    for d in range(nt):
        f = lax.rem(z + nt - d, nt)
        sib_copies[d].wait_recv()
        far_copies[d].wait_recv()
        cols = pl.ds(pl.multiple_of(f * dt, LANES), dt)
        part = lax.dot_general(
            cot[f].reshape(ne * tok, dt), w[:, cols], (((1,), (1,)), ((), ())),
            preferred_element_type=F32,
        )
        if d == 0:
            back[...] = part
        else:
            back[...] += part

    sg_part[...] = lax.dot_general(
        cot[e].reshape(ne * tok, dt), sw[...], (((1,), (1,)), ((), ())),
        preferred_element_type=F32,
    ).reshape(ne, tok, hs)
    for g in range(2):
        sg_out[g] = sg_part[order[g]].astype(BF16)
    sg = send(sg_out, sg_in, {"expert": sib})

    def reduce_z(s):
        s2[s].wait_recv()
        s3_out[s] = (keep[s, 1] + s2_in[s].astype(F32)).astype(BF16)
        to = {"phase": ahead, "tensor": others_t[s] if s < nt - 1 else z}
        s3.append(send(s3_out.at[s], s3_in.at[s], to))

    def rows_back(i):
        x = e * here + i
        at = [pack[b, pl.ds(x, 1), :][:, tok:] for b in range(ne)]
        named = jnp.concatenate([a * ne + b for b, a in enumerate(at)], axis=1)
        entry_down = lax.broadcasted_iota(jnp.int32, (slots_all, ne * tok), 0).astype(F32)
        place = jnp.where(named == entry_down, 1.0, 0.0).astype(BF16)
        gates = jnp.concatenate([pick(pack[b].T[tok:], experts + x) for b in range(ne)], axis=0)
        rows = (back[:, i * hq:(i + 1) * hq] * gates).astype(BF16)
        hgrad_ref[i] = jnp.dot(place, rows, preferred_element_type=F32).astype(BF16).reshape(
            cap, ne, hq
        )

    reduce_z(0)
    rows_back(0)
    sg.wait_recv()
    sg_out2[...] = (sg_part[far] + sg_in[0].astype(F32)).astype(BF16)
    sg2 = send(sg_out2, sg_in2, {"expert": far})
    reduce_z(1)
    for i in range(1, here):
        rows_back(i)
    for s in range(2, nt):
        reduce_z(s)
    sg2.wait_recv()
    sgrad_ref[...] = (
        sg_part[e] + sg_in[1].astype(F32) + sg_in2[...].astype(F32)
    ).astype(BF16)
    total = jnp.zeros(next_ref.shape, F32)
    for s in range(nt):
        s3[s].wait_recv()
        total = total + s3_in[s].astype(F32)
    next_ref[...] = total.astype(BF16)
    for copy in copies:
        copy.wait_send()


def store_kernel(*refs):
    count = len(refs) // 2
    sems = refs[-1]
    moves = [
        pltpu.make_async_copy(refs[i], refs[count + i], sems.at[i]) for i in range(count)
    ]
    for move in moves:
        move.start()
    for move in moves:
        move.wait()


def fused(sizes, fr, fg, hidden, weight, shared, sweight, br, bg, cot):
    phases, ne, nt = sizes
    here, groups, cap, hq = hidden.shape[1:]
    tok, top = fr.shape[1:]
    features = weight.shape[3]
    dt = cot.shape[2]
    hs = shared.shape[2]
    vmem = pl.BlockSpec(memory_space=pltpu.VMEM)
    hbm = pl.BlockSpec(memory_space=pltpu.HBM)
    copies = 6 + (nt - 1) + 6 * nt + 2
    rows = ne * tok
    results = (
        jax.ShapeDtypeStruct((tok, dt), BF16),
        jax.ShapeDtypeStruct((here, cap, groups, hq), BF16),
        jax.ShapeDtypeStruct((tok, hs), BF16),
    )
    made = pl.pallas_call(
        functools.partial(fused_kernel, sizes),
        out_shape=results,
        in_specs=[hbm] * 9,
        out_specs=(vmem, vmem, vmem),
        scratch_shapes=[
            pltpu.VMEM((top, 1, tok), jnp.int32),
            pltpu.VMEM((top, 1, tok), F32),
            pltpu.VMEM((top, 1, tok), jnp.int32),
            pltpu.VMEM((top, 1, tok), F32),
            pltpu.VMEM((here, cap, groups, hq), BF16),
            pltpu.VMEM((here * hq, features), BF16),
            pltpu.VMEM((hs, dt), BF16),
            pltpu.VMEM((ne, tok, hs), BF16),
            pltpu.VMEM((nt, ne, tok, dt), BF16),
            pltpu.VMEM((ne, 2 * here * ne, 2 * tok), F32),
            pltpu.VMEM((rows, here * hq), BF16),
            pltpu.VMEM((rows, dt), F32),
            pltpu.VMEM((nt, 2, tok, dt), F32),
            pltpu.VMEM((nt, 2, tok, dt), BF16),
            pltpu.VMEM((nt, 2, tok, dt), BF16),
            pltpu.VMEM((nt, tok, dt), BF16),
            pltpu.VMEM((nt, tok, dt), BF16),
            pltpu.VMEM((nt, tok, dt), BF16),
            pltpu.VMEM((nt, tok, dt), BF16),
            pltpu.VMEM((rows, here * hq), F32),
            pltpu.VMEM((ne, tok, hs), F32),
            pltpu.VMEM((2, tok, hs), BF16),
            pltpu.VMEM((2, tok, hs), BF16),
            pltpu.VMEM((tok, hs), BF16),
            pltpu.VMEM((tok, hs), BF16),
            pltpu.SemaphoreType.DMA((copies,)),
            pltpu.SemaphoreType.DMA((copies,)),
            pltpu.SemaphoreType.DMA((9,)),
        ],
        compiler_params=pltpu.CompilerParams(
            collective_id=0, has_side_effects=True, vmem_limit_bytes=32 * 1024 * 1024
        ),
    )(
        *(a.transpose(2, 0, 1) for a in (fr, fg, br, bg)),
        hidden[0].transpose(0, 2, 1, 3),
        weight.reshape(here * hq, features),
        shared[0], sweight[0], cot[0],
    )
    handed, hgrad, sgrad = pl.pallas_call(
        store_kernel,
        out_shape=results,
        in_specs=[vmem] * 3,
        out_specs=[hbm] * 3,
        scratch_shapes=[pltpu.SemaphoreType.DMA((3,))],
    )(*made)
    return handed[None], hgrad.transpose(0, 2, 1, 3)[None], sgrad[None]


def shifted(value, axis, steps):
    count = lax.axis_size(axis)
    pairs = [(source, (source + steps) % count) for source in range(count)]
    return lax.ppermute(value, axis, pairs)


def slot_numbers(routes, experts):
    numbers = jnp.arange(experts, dtype=jnp.int32)
    onehot = (routes[:, :, None] == numbers[None, None, :]).astype(jnp.int32)
    per_token = jnp.sum(onehot, axis=1)
    before = jnp.cumsum(per_token, axis=0) - per_token
    return jnp.sum(onehot * before[:, None, :], axis=2)


def row_positions(routes, experts_here, groups, capacity):
    slot_index = slot_numbers(routes, experts_here * groups)
    holder = routes // experts_here
    within = routes - holder * experts_here
    return ((within * groups + holder) * capacity + slot_index).reshape(-1)


def place_rows(gates, values, positions, total_rows):
    scaled = (gates[:, :, None] * values[:, None, :].astype(jnp.float32)).astype(jnp.bfloat16)
    outgoing = jnp.zeros((total_rows, values.shape[1]), jnp.bfloat16)
    return outgoing.at[positions].set(scaled.reshape(-1, values.shape[1]))


def unfused(
    forward_routes,
    forward_gates,
    hidden_rows,
    down_weight,
    shared_hidden,
    shared_weight,
    backward_routes,
    backward_gates,
    cotangent,
):
    experts_here = down_weight.shape[1]
    features = down_weight.shape[3]
    capacity = hidden_rows.shape[3]
    groups = lax.axis_size("expert")
    token_count = forward_routes.shape[1]
    top_count = forward_routes.shape[2]
    hidden = hidden_rows[0]
    weight = down_weight[0]
    local_shared = shared_hidden[0]
    shared_piece = shared_weight[0]
    shared_part = jnp.dot(
        local_shared,
        lax.all_gather(shared_piece, "expert", axis=1, tiled=True),
        preferred_element_type=jnp.float32,
    )
    fore_positions = row_positions(forward_routes[0], experts_here, groups, capacity)
    fore_gates = forward_gates[0]
    partial_value = jnp.einsum(
        "egmh,ehd->egmd", hidden, weight, preferred_element_type=jnp.float32
    ).astype(jnp.bfloat16)
    arrived = lax.all_to_all(partial_value, "expert", split_axis=1, concat_axis=1, tiled=True)
    picked = arrived.reshape(-1, features)[fore_positions].reshape(token_count, top_count, features)
    summand = shared_part + jnp.sum(picked.astype(jnp.float32) * fore_gates[:, :, None], axis=1)
    summed = lax.psum_scatter(summand, "tensor", scatter_dimension=1, tiled=True)
    layer_out = summed.astype(jnp.bfloat16)
    handed = shifted(layer_out, "phase", 1)
    cotangent_whole = lax.all_gather(cotangent[0], "tensor", axis=1, tiled=True)
    back_positions = row_positions(backward_routes[0], experts_here, groups, capacity)
    total_rows = experts_here * groups * capacity
    outgoing = place_rows(backward_gates[0], cotangent_whole, back_positions, total_rows)
    received = lax.all_to_all(
        outgoing.reshape(experts_here, groups, capacity, features),
        "expert",
        split_axis=1,
        concat_axis=1,
        tiled=True,
    )
    hidden_back = jnp.einsum(
        "egmd,ehd->egmh", received, weight, preferred_element_type=jnp.float32
    ).astype(jnp.bfloat16)
    shared_back = lax.dot_general(
        cotangent_whole,
        lax.all_gather(shared_piece, "expert", axis=1, tiled=True),
        (((1,), (1,)), ((), ())),
        preferred_element_type=jnp.float32,
    )
    return (handed[None], hidden_back[None], shared_back.astype(jnp.bfloat16)[None])


def solution(mesh):
    sizes = tuple(mesh.shape[axis] for axis in ("phase", "expert", "tensor"))

    def on_device(*arrays):
        phases, ne, nt = sizes
        hidden, weight, cot = arrays[2], arrays[3], arrays[8]
        two_chips = ne == 4 and ne == nt and phases > 1
        fits = 2 * arrays[0].shape[1] <= LANES and cot.shape[2] % LANES == 0
        if two_chips and fits:
            return fused(sizes, *arrays)
        return unfused(*arrays)

    return jax.shard_map(
        on_device,
        mesh=mesh,
        in_specs=(
            P("phase", "expert", None),
            P("phase", "expert", None),
            P("phase", "expert", None, None, "tensor"),
            P("phase", "expert", "tensor", None),
            P("phase", "expert", "tensor"),
            P("phase", "tensor", "expert"),
            P("phase", "expert", None),
            P("phase", "expert", None),
            P("phase", "expert", "tensor"),
        ),
        out_specs=(
            P("phase", "expert", "tensor"),
            P("phase", "expert", None, None, "tensor"),
            P("phase", "expert", "tensor"),
        ),
        check_vma=False,
    )
```

```python
import functools

import jax
import jax.numpy as jnp
from jax import lax
from jax.experimental import pallas as pl
from jax.experimental.pallas import tpu as pltpu
from jax.sharding import PartitionSpec as P

MESH = pl.DeviceIdType.MESH
LANES = 128
F32 = jnp.float32
BF16 = jnp.bfloat16


def fused_kernel(
    sizes,
    fr_hbm, fg_hbm, br_hbm, bg_hbm,
    hid_hbm, w_hbm, sh_hbm, sw_hbm, cot_hbm,
    next_ref, hgrad_ref, sgrad_ref,
    fr, fg, br, bg,
    hid, w, sw, sh, cot, pack, hc, acc, keep,
    s1_out, s1_in, s2_out, s2_in, s3_out, s3_in,
    back, sg_part, sg_out, sg_in, sg_out2, sg_in2,
    send_sem, recv_sem, load_sem,
):
    phases, ne, nt = sizes
    ph, e, z = lax.axis_index("phase"), lax.axis_index("expert"), lax.axis_index("tensor")
    top, _, tok = fr.shape
    here, cap, _, hq = hid.shape
    dt = cot.shape[3]
    hs = sw.shape[0]
    experts = here * ne
    slots_all = cap * ne
    core = lax.rem(e, 2)
    sib = e + 1 - 2 * core
    far = lax.rem(e + 2, ne)
    far_sib = lax.rem(sib + 2, ne)
    others_t = [lax.rem(z + d, nt) for d in range(1, nt)]
    ahead, behind = lax.rem(ph + 1, phases), lax.rem(ph + phases - 1, phases)

    pairs = (
        (fr_hbm, fr), (fg_hbm, fg), (br_hbm, br), (bg_hbm, bg),
        (cot_hbm, cot.at[z, e]), (sh_hbm, sh.at[e]), (hid_hbm, hid), (w_hbm, w), (sw_hbm, sw),
    )
    loads = [pltpu.make_async_copy(a, b, load_sem.at[i]) for i, (a, b) in enumerate(pairs)]
    for load in loads:
        load.start()

    barrier = pltpu.get_barrier_semaphore()
    partners = [{"expert": sib}, {"expert": far}] + [{"tensor": o} for o in others_t]
    for step in range(nt):
        partners.append({"phase": ahead, "tensor": lax.rem(z + step, nt)})
        if phases > 2:
            partners.append({"phase": behind, "tensor": lax.rem(z + step, nt)})
    for partner in partners:
        pl.semaphore_signal(barrier, inc=1, device_id=partner, device_id_type=MESH)

    for load in loads[:4]:
        load.wait()
    across = 2 * experts
    level = lax.broadcasted_iota(jnp.int32, (across, 2 * tok), 0)
    hot = jnp.zeros((across, 2 * tok), F32)
    gate = jnp.zeros((across, 2 * tok), F32)
    for k in range(top):
        named = jnp.concatenate([fr[k], br[k]], axis=1)
        weigh = jnp.concatenate([fg[k], bg[k]], axis=1)
        hot = jnp.where(named == level, 1.0, hot)
        gate = jnp.where(named + experts == level, weigh, gate)
    first = lax.broadcasted_iota(jnp.int32, (2 * tok, 2 * tok), 0)
    second = lax.broadcasted_iota(jnp.int32, (2 * tok, 2 * tok), 1)
    earlier = (first < second) & ((first < tok) == (second < tok))
    counts = jnp.dot(
        hot.astype(BF16), jnp.where(earlier, 1.0, 0.0).astype(BF16), preferred_element_type=F32
    )
    pack[e] = jnp.where(level < experts, jnp.where(hot > 0.5, counts, -1.0), gate)

    copies = []

    def send(src, dst, to):
        i = len(copies)
        copy = pltpu.make_async_remote_copy(
            src_ref=src, dst_ref=dst, send_sem=send_sem.at[i], recv_sem=recv_sem.at[i],
            device_id=to, device_id_type=MESH,
        )
        copy.start()
        copies.append(copy)
        return copy

    def spread(buffer):
        return [send(buffer.at[e], buffer.at[e], {"expert": o}) for o in (far, sib)]

    def hand_on(buffer, pair):
        pair[0].wait_recv()
        pair.append(send(buffer.at[far], buffer.at[far], {"expert": sib}))

    pl.semaphore_wait(barrier, len(partners))
    pack_copies = spread(pack)
    loads[5].wait()
    sh_copies = spread(sh)
    loads[4].wait()
    mine = cot.at[z, e]
    z_copies = [send(mine, mine, {"tensor": o}) for o in others_t]
    y_copies = [send(mine, mine, {"expert": far})]
    sib_copies = [send(mine, mine, {"expert": sib})]
    hand_on(pack, pack_copies)
    hand_on(sh, sh_copies)

    order = (far_sib, sib, far, e)
    level = lax.broadcasted_iota(jnp.int32, (tok, across), 1)
    entry = lax.broadcasted_iota(jnp.int32, (tok, slots_all), 1).astype(F32)

    def pick(table, at):
        return jnp.sum(jnp.where(level == at, table, 0.0), axis=1, keepdims=True)

    pack_copies[1].wait_recv()
    pack_copies[2].wait_recv()
    loads[6].wait()
    hidden = [hid[i].reshape(slots_all, hq) for i in range(here)]
    for n, b in enumerate(order):
        table = pack[b].T[:tok]
        offset = b.astype(F32)
        for i in range(here):
            x = e * here + i
            place = jnp.where(pick(table, x) * ne + offset == entry, 1.0, 0.0).astype(BF16)
            rows = jnp.dot(place, hidden[i], preferred_element_type=F32)
            hc[n * tok:(n + 1) * tok, i * hq:(i + 1) * hq] = (
                rows * pick(table, experts + x)
            ).astype(BF16)

    def relay(d):
        z_copies[d - 1].wait_recv()
        piece = cot.at[lax.rem(z + nt - d, nt), e]
        y_copies.append(send(piece, piece, {"expert": far}))
        sib_copies.append(send(piece, piece, {"expert": sib}))

    relay(1)
    loads[7].wait()
    loads[8].wait()
    sh_copies[1].wait_recv()
    sh_copies[2].wait_recv()
    s1, s2, s3 = [], [], []
    for s in range(nt):
        f = lax.rem(z + 1 + s, nt)
        cols = pl.ds(pl.multiple_of(f * dt, LANES), dt)
        acc[...] = jnp.dot(hc[...], w[:, cols], preferred_element_type=F32)

        @pl.when(f == e)
        def _():
            shared = jnp.concatenate([sh[b] for b in order], axis=0)
            acc[...] += jnp.dot(shared, sw[...], preferred_element_type=F32)

        for g in range(2):
            s1_out[s, g] = acc[g * tok:(g + 1) * tok, :].astype(BF16)
        s1.append(send(s1_out.at[s], s1_in.at[s], {"expert": sib}))
        for g in range(2):
            keep[s, g] = acc[(2 + g) * tok:(3 + g) * tok, :]
        if 1 <= s < nt - 1:
            relay(s + 1)
    for s in range(nt):
        s1[s].wait_recv()
        s2_out[s] = (keep[s, 0] + s1_in[s, 0].astype(F32)).astype(BF16)
        s2.append(send(s2_out.at[s], s2_in.at[s], {"expert": far}))
        keep[s, 1] = keep[s, 1] + s1_in[s, 1].astype(F32)

    far_copies = []
    for d in range(nt):
        y_copies[d].wait_recv()
        piece = cot.at[lax.rem(z + nt - d, nt), far]
        far_copies.append(send(piece, piece, {"expert": sib}))

    for d in range(nt):
        f = lax.rem(z + nt - d, nt)
        sib_copies[d].wait_recv()
        far_copies[d].wait_recv()
        cols = pl.ds(pl.multiple_of(f * dt, LANES), dt)
        part = lax.dot_general(
            cot[f].reshape(ne * tok, dt), w[:, cols], (((1,), (1,)), ((), ())),
            preferred_element_type=F32,
        )
        if d == 0:
            back[...] = part
        else:
            back[...] += part

    sg_part[...] = lax.dot_general(
        cot[e].reshape(ne * tok, dt), sw[...], (((1,), (1,)), ((), ())),
        preferred_element_type=F32,
    ).reshape(ne, tok, hs)
    for g in range(2):
        sg_out[g] = sg_part[order[g]].astype(BF16)
    sg = send(sg_out, sg_in, {"expert": sib})

    def reduce_z(s):
        s2[s].wait_recv()
        s3_out[s] = (keep[s, 1] + s2_in[s].astype(F32)).astype(BF16)
        to = {"phase": ahead, "tensor": others_t[s] if s < nt - 1 else z}
        s3.append(send(s3_out.at[s], s3_in.at[s], to))

    def rows_back(i):
        x = e * here + i
        at = [pack[b, pl.ds(x, 1), :][:, tok:] for b in range(ne)]
        named = jnp.concatenate([a * ne + b for b, a in enumerate(at)], axis=1)
        entry_down = lax.broadcasted_iota(jnp.int32, (slots_all, ne * tok), 0).astype(F32)
        place = jnp.where(named == entry_down, 1.0, 0.0).astype(BF16)
        gates = jnp.concatenate([pick(pack[b].T[tok:], experts + x) for b in range(ne)], axis=0)
        rows = (back[:, i * hq:(i + 1) * hq] * gates).astype(BF16)
        hgrad_ref[i] = jnp.dot(place, rows, preferred_element_type=F32).astype(BF16).reshape(
            cap, ne, hq
        )

    reduce_z(0)
    rows_back(0)
    sg.wait_recv()
    sg_out2[...] = (sg_part[far] + sg_in[0].astype(F32)).astype(BF16)
    sg2 = send(sg_out2, sg_in2, {"expert": far})
    reduce_z(1)
    for i in range(1, here):
        rows_back(i)
    for s in range(2, nt):
        reduce_z(s)
    sg2.wait_recv()
    sgrad_ref[...] = (
        sg_part[e] + sg_in[1].astype(F32) + sg_in2[...].astype(F32)
    ).astype(BF16)
    total = jnp.zeros(next_ref.shape, F32)
    for s in range(nt):
        s3[s].wait_recv()
        total = total + s3_in[s].astype(F32)
    next_ref[...] = total.astype(BF16)
    for copy in copies:
        copy.wait_send()


def store_kernel(*refs):
    count = len(refs) // 2
    sems = refs[-1]
    moves = [
        pltpu.make_async_copy(refs[i], refs[count + i], sems.at[i]) for i in range(count)
    ]
    for move in moves:
        move.start()
    for move in moves:
        move.wait()


def fused(sizes, fr, fg, hidden, weight, shared, sweight, br, bg, cot):
    phases, ne, nt = sizes
    here, groups, cap, hq = hidden.shape[1:]
    tok, top = fr.shape[1:]
    features = weight.shape[3]
    dt = cot.shape[2]
    hs = shared.shape[2]
    vmem = pl.BlockSpec(memory_space=pltpu.VMEM)
    hbm = pl.BlockSpec(memory_space=pltpu.HBM)
    copies = 6 + (nt - 1) + 6 * nt + 2
    rows = ne * tok
    results = (
        jax.ShapeDtypeStruct((tok, dt), BF16),
        jax.ShapeDtypeStruct((here, cap, groups, hq), BF16),
        jax.ShapeDtypeStruct((tok, hs), BF16),
    )
    made = pl.pallas_call(
        functools.partial(fused_kernel, sizes),
        out_shape=results,
        in_specs=[hbm] * 9,
        out_specs=(vmem, vmem, vmem),
        scratch_shapes=[
            pltpu.VMEM((top, 1, tok), jnp.int32),
            pltpu.VMEM((top, 1, tok), F32),
            pltpu.VMEM((top, 1, tok), jnp.int32),
            pltpu.VMEM((top, 1, tok), F32),
            pltpu.VMEM((here, cap, groups, hq), BF16),
            pltpu.VMEM((here * hq, features), BF16),
            pltpu.VMEM((hs, dt), BF16),
            pltpu.VMEM((ne, tok, hs), BF16),
            pltpu.VMEM((nt, ne, tok, dt), BF16),
            pltpu.VMEM((ne, 2 * here * ne, 2 * tok), F32),
            pltpu.VMEM((rows, here * hq), BF16),
            pltpu.VMEM((rows, dt), F32),
            pltpu.VMEM((nt, 2, tok, dt), F32),
            pltpu.VMEM((nt, 2, tok, dt), BF16),
            pltpu.VMEM((nt, 2, tok, dt), BF16),
            pltpu.VMEM((nt, tok, dt), BF16),
            pltpu.VMEM((nt, tok, dt), BF16),
            pltpu.VMEM((nt, tok, dt), BF16),
            pltpu.VMEM((nt, tok, dt), BF16),
            pltpu.VMEM((rows, here * hq), F32),
            pltpu.VMEM((ne, tok, hs), F32),
            pltpu.VMEM((2, tok, hs), BF16),
            pltpu.VMEM((2, tok, hs), BF16),
            pltpu.VMEM((tok, hs), BF16),
            pltpu.VMEM((tok, hs), BF16),
            pltpu.SemaphoreType.DMA((copies,)),
            pltpu.SemaphoreType.DMA((copies,)),
            pltpu.SemaphoreType.DMA((9,)),
        ],
        compiler_params=pltpu.CompilerParams(
            collective_id=0, has_side_effects=True, vmem_limit_bytes=32 * 1024 * 1024
        ),
    )(
        *(
            pltpu.with_memory_space_constraint(a, pltpu.HBM)
            for a in (
                *(r.transpose(2, 0, 1) for r in (fr, fg, br, bg)),
                hidden[0].transpose(0, 2, 1, 3),
                weight.reshape(here * hq, features),
                shared[0], sweight[0], cot[0],
            )
        )
    )
    handed, hgrad, sgrad = pl.pallas_call(
        store_kernel,
        out_shape=results,
        in_specs=[vmem] * 3,
        out_specs=[hbm] * 3,
        scratch_shapes=[pltpu.SemaphoreType.DMA((3,))],
        compiler_params=pltpu.CompilerParams(vmem_limit_bytes=4 * 1024 * 1024),
    )(*made)
    return handed[None], hgrad.transpose(0, 2, 1, 3)[None], sgrad[None]


def shifted(value, axis, steps):
    count = lax.axis_size(axis)
    pairs = [(source, (source + steps) % count) for source in range(count)]
    return lax.ppermute(value, axis, pairs)


def slot_numbers(routes, experts):
    numbers = jnp.arange(experts, dtype=jnp.int32)
    onehot = (routes[:, :, None] == numbers[None, None, :]).astype(jnp.int32)
    per_token = jnp.sum(onehot, axis=1)
    before = jnp.cumsum(per_token, axis=0) - per_token
    return jnp.sum(onehot * before[:, None, :], axis=2)


def row_positions(routes, experts_here, groups, capacity):
    slot_index = slot_numbers(routes, experts_here * groups)
    holder = routes // experts_here
    within = routes - holder * experts_here
    return ((within * groups + holder) * capacity + slot_index).reshape(-1)


def place_rows(gates, values, positions, total_rows):
    scaled = (gates[:, :, None] * values[:, None, :].astype(jnp.float32)).astype(jnp.bfloat16)
    outgoing = jnp.zeros((total_rows, values.shape[1]), jnp.bfloat16)
    return outgoing.at[positions].set(scaled.reshape(-1, values.shape[1]))


def unfused(
    forward_routes,
    forward_gates,
    hidden_rows,
    down_weight,
    shared_hidden,
    shared_weight,
    backward_routes,
    backward_gates,
    cotangent,
):
    experts_here = down_weight.shape[1]
    features = down_weight.shape[3]
    capacity = hidden_rows.shape[3]
    groups = lax.axis_size("expert")
    token_count = forward_routes.shape[1]
    top_count = forward_routes.shape[2]
    hidden = hidden_rows[0]
    weight = down_weight[0]
    local_shared = shared_hidden[0]
    shared_piece = shared_weight[0]
    shared_part = jnp.dot(
        local_shared,
        lax.all_gather(shared_piece, "expert", axis=1, tiled=True),
        preferred_element_type=jnp.float32,
    )
    fore_positions = row_positions(forward_routes[0], experts_here, groups, capacity)
    fore_gates = forward_gates[0]
    partial_value = jnp.einsum(
        "egmh,ehd->egmd", hidden, weight, preferred_element_type=jnp.float32
    ).astype(jnp.bfloat16)
    arrived = lax.all_to_all(partial_value, "expert", split_axis=1, concat_axis=1, tiled=True)
    picked = arrived.reshape(-1, features)[fore_positions].reshape(token_count, top_count, features)
    summand = shared_part + jnp.sum(picked.astype(jnp.float32) * fore_gates[:, :, None], axis=1)
    summed = lax.psum_scatter(summand, "tensor", scatter_dimension=1, tiled=True)
    layer_out = summed.astype(jnp.bfloat16)
    handed = shifted(layer_out, "phase", 1)
    cotangent_whole = lax.all_gather(cotangent[0], "tensor", axis=1, tiled=True)
    back_positions = row_positions(backward_routes[0], experts_here, groups, capacity)
    total_rows = experts_here * groups * capacity
    outgoing = place_rows(backward_gates[0], cotangent_whole, back_positions, total_rows)
    received = lax.all_to_all(
        outgoing.reshape(experts_here, groups, capacity, features),
        "expert",
        split_axis=1,
        concat_axis=1,
        tiled=True,
    )
    hidden_back = jnp.einsum(
        "egmd,ehd->egmh", received, weight, preferred_element_type=jnp.float32
    ).astype(jnp.bfloat16)
    shared_back = lax.dot_general(
        cotangent_whole,
        lax.all_gather(shared_piece, "expert", axis=1, tiled=True),
        (((1,), (1,)), ((), ())),
        preferred_element_type=jnp.float32,
    )
    return (handed[None], hidden_back[None], shared_back.astype(jnp.bfloat16)[None])


def solution(mesh):
    sizes = tuple(mesh.shape[axis] for axis in ("phase", "expert", "tensor"))

    def on_device(*arrays):
        phases, ne, nt = sizes
        hidden, weight, cot = arrays[2], arrays[3], arrays[8]
        two_chips = ne == 4 and ne == nt and phases > 1
        fits = 2 * arrays[0].shape[1] <= LANES and cot.shape[2] % LANES == 0
        if two_chips and fits:
            return fused(sizes, *arrays)
        return unfused(*arrays)

    return jax.shard_map(
        on_device,
        mesh=mesh,
        in_specs=(
            P("phase", "expert", None),
            P("phase", "expert", None),
            P("phase", "expert", None, None, "tensor"),
            P("phase", "expert", "tensor", None),
            P("phase", "expert", "tensor"),
            P("phase", "tensor", "expert"),
            P("phase", "expert", None),
            P("phase", "expert", None),
            P("phase", "expert", "tensor"),
        ),
        out_specs=(
            P("phase", "expert", "tensor"),
            P("phase", "expert", None, None, "tensor"),
            P("phase", "expert", "tensor"),
        ),
        check_vma=False,
    )
```

```python
import functools

import jax
import jax.numpy as jnp
from jax import lax
from jax.experimental import pallas as pl
from jax.experimental.pallas import tpu as pltpu
from jax.sharding import PartitionSpec as P

MESH = pl.DeviceIdType.MESH
LANES = 128
F32 = jnp.float32
BF16 = jnp.bfloat16


def fused_kernel(
    sizes,
    fr_hbm, fg_hbm, br_hbm, bg_hbm,
    hid_hbm, w_hbm, sh_hbm, sw_hbm, cot_hbm,
    next_ref, hgrad_ref, sgrad_ref,
    fr, fg, br, bg,
    hid, w, sw, sh, cot, pack, hc, acc, keep,
    s1_out, s1_in, s2_out, s2_in, s3_out, s3_in,
    back, sg_part, sg_out, sg_in, sg_out2, sg_in2,
    send_sem, recv_sem, load_sem,
):
    phases, ne, nt = sizes
    ph, e, z = lax.axis_index("phase"), lax.axis_index("expert"), lax.axis_index("tensor")
    top, _, tok = fr.shape
    here, cap, _, hq = hid.shape
    dt = cot.shape[3]
    hs = sw.shape[0]
    experts = here * ne
    slots_all = cap * ne
    core = lax.rem(e, 2)
    sib = e + 1 - 2 * core
    far = lax.rem(e + 2, ne)
    far_sib = lax.rem(sib + 2, ne)
    others_t = [lax.rem(z + d, nt) for d in range(1, nt)]
    ahead, behind = lax.rem(ph + 1, phases), lax.rem(ph + phases - 1, phases)

    pairs = (
        (fr_hbm, fr), (fg_hbm, fg), (br_hbm, br), (bg_hbm, bg),
        (cot_hbm, cot.at[z, e]), (sh_hbm, sh.at[e]), (hid_hbm, hid), (w_hbm, w), (sw_hbm, sw),
    )
    loads = [pltpu.make_async_copy(a, b, load_sem.at[i]) for i, (a, b) in enumerate(pairs)]
    for load in loads:
        load.start()

    barrier = pltpu.get_barrier_semaphore()
    partners = [{"expert": sib}, {"expert": far}] + [{"tensor": o} for o in others_t]
    for step in range(nt):
        partners.append({"phase": ahead, "tensor": lax.rem(z + step, nt)})
        if phases > 2:
            partners.append({"phase": behind, "tensor": lax.rem(z + step, nt)})
    for partner in partners:
        pl.semaphore_signal(barrier, inc=1, device_id=partner, device_id_type=MESH)

    copies = []

    def send(src, dst, to):
        i = len(copies)
        copy = pltpu.make_async_remote_copy(
            src_ref=src, dst_ref=dst, send_sem=send_sem.at[i], recv_sem=recv_sem.at[i],
            device_id=to, device_id_type=MESH,
        )
        copy.start()
        copies.append(copy)
        return copy

    def spread(buffer):
        return [send(buffer.at[e], buffer.at[e], {"expert": o}) for o in (far, sib)]

    def hand_on(buffer, pair):
        pair[0].wait_recv()
        pair.append(send(buffer.at[far], buffer.at[far], {"expert": sib}))

    pl.semaphore_wait(barrier, len(partners))
    loads[4].wait()
    mine = cot.at[z, e]
    z_copies = [send(mine, mine, {"tensor": o}) for o in others_t]
    loads[5].wait()
    sh_copies = spread(sh)
    y_copies, sib_copies, far_copies = [], [], []

    for load in loads[:4]:
        load.wait()
    across = 2 * experts
    level = lax.broadcasted_iota(jnp.int32, (across, 2 * tok), 0)
    hot = jnp.zeros((across, 2 * tok), F32)
    gate = jnp.zeros((across, 2 * tok), F32)
    for k in range(top):
        named = jnp.concatenate([fr[k], br[k]], axis=1)
        weigh = jnp.concatenate([fg[k], bg[k]], axis=1)
        hot = jnp.where(named == level, 1.0, hot)
        gate = jnp.where(named + experts == level, weigh, gate)
    first = lax.broadcasted_iota(jnp.int32, (2 * tok, 2 * tok), 0)
    second = lax.broadcasted_iota(jnp.int32, (2 * tok, 2 * tok), 1)
    earlier = (first < second) & ((first < tok) == (second < tok))
    counts = jnp.dot(
        hot.astype(BF16), jnp.where(earlier, 1.0, 0.0).astype(BF16), preferred_element_type=F32
    )
    pack[e] = jnp.where(level < experts, jnp.where(hot > 0.5, counts, -1.0), gate)

    pack_copies = spread(pack)
    y_copies.append(send(mine, mine, {"expert": far}))
    sib_copies.append(send(mine, mine, {"expert": sib}))
    hand_on(sh, sh_copies)
    hand_on(pack, pack_copies)

    order = (far_sib, sib, far, e)
    level = lax.broadcasted_iota(jnp.int32, (tok, across), 1)
    entry = lax.broadcasted_iota(jnp.int32, (tok, slots_all), 1).astype(F32)

    def pick(table, at):
        return jnp.sum(jnp.where(level == at, table, 0.0), axis=1, keepdims=True)

    pack_copies[1].wait_recv()
    pack_copies[2].wait_recv()
    loads[6].wait()
    hidden = [hid[i].reshape(slots_all, hq) for i in range(here)]
    for n, b in enumerate(order):
        table = pack[b].T[:tok]
        offset = b.astype(F32)
        for i in range(here):
            x = e * here + i
            place = jnp.where(pick(table, x) * ne + offset == entry, 1.0, 0.0).astype(BF16)
            rows = jnp.dot(place, hidden[i], preferred_element_type=F32)
            hc[n * tok:(n + 1) * tok, i * hq:(i + 1) * hq] = (
                rows * pick(table, experts + x)
            ).astype(BF16)

    def relay(d):
        z_copies[d - 1].wait_recv()
        piece = cot.at[lax.rem(z + nt - d, nt), e]
        y_copies.append(send(piece, piece, {"expert": far}))
        sib_copies.append(send(piece, piece, {"expert": sib}))

    relay(1)
    loads[7].wait()
    loads[8].wait()
    sh_copies[1].wait_recv()
    sh_copies[2].wait_recv()
    s1, s2, s3 = [], [], []
    for s in range(nt):
        f = lax.rem(z + 1 + s, nt)
        cols = pl.ds(pl.multiple_of(f * dt, LANES), dt)
        acc[...] = jnp.dot(hc[...], w[:, cols], preferred_element_type=F32)

        @pl.when(f == e)
        def _():
            shared = jnp.concatenate([sh[b] for b in order], axis=0)
            acc[...] += jnp.dot(shared, sw[...], preferred_element_type=F32)

        for g in range(2):
            s1_out[s, g] = acc[g * tok:(g + 1) * tok, :].astype(BF16)
        s1.append(send(s1_out.at[s], s1_in.at[s], {"expert": sib}))
        for g in range(2):
            keep[s, g] = acc[(2 + g) * tok:(3 + g) * tok, :]

    def reduce_core(s):
        s1[s].wait_recv()
        s2_out[s] = (keep[s, 0] + s1_in[s, 0].astype(F32)).astype(BF16)
        s2.append(send(s2_out.at[s], s2_in.at[s], {"expert": far}))
        keep[s, 1] = keep[s, 1] + s1_in[s, 1].astype(F32)

    def hand_over(d):
        y_copies[d].wait_recv()
        piece = cot.at[lax.rem(z + nt - d, nt), far]
        far_copies.append(send(piece, piece, {"expert": sib}))

    def back_part(d):
        f = lax.rem(z + nt - d, nt)
        sib_copies[d].wait_recv()
        far_copies[d].wait_recv()
        cols = pl.ds(pl.multiple_of(f * dt, LANES), dt)
        part = lax.dot_general(
            cot[f].reshape(ne * tok, dt), w[:, cols], (((1,), (1,)), ((), ())),
            preferred_element_type=F32,
        )
        if d == 0:
            back[...] = part
        else:
            back[...] += part

    def reduce_z(s):
        s2[s].wait_recv()
        s3_out[s] = (keep[s, 1] + s2_in[s].astype(F32)).astype(BF16)
        to = {"phase": ahead, "tensor": others_t[s] if s < nt - 1 else z}
        s3.append(send(s3_out.at[s], s3_in.at[s], to))

    def rows_back(i):
        x = e * here + i
        at = [pack[b, pl.ds(x, 1), :][:, tok:] for b in range(ne)]
        named = jnp.concatenate([a * ne + b for b, a in enumerate(at)], axis=1)
        entry_down = lax.broadcasted_iota(jnp.int32, (slots_all, ne * tok), 0).astype(F32)
        place = jnp.where(named == entry_down, 1.0, 0.0).astype(BF16)
        gates = jnp.concatenate([pick(pack[b].T[tok:], experts + x) for b in range(ne)], axis=0)
        rows = (back[:, i * hq:(i + 1) * hq] * gates).astype(BF16)
        hgrad_ref[i] = jnp.dot(place, rows, preferred_element_type=F32).astype(BF16).reshape(
            cap, ne, hq
        )

    half = nt // 2
    for s in range(half):
        reduce_core(s)
    for d in range(half):
        hand_over(d)
    for d in range(2, nt):
        relay(d)
    for s in range(half, nt):
        reduce_core(s)
    for d in range(half):
        back_part(d)
    for s in range(half):
        reduce_z(s)
    for d in range(half, nt):
        hand_over(d)
    for d in range(half, nt):
        back_part(d)

    sg_part[...] = lax.dot_general(
        cot[e].reshape(ne * tok, dt), sw[...], (((1,), (1,)), ((), ())),
        preferred_element_type=F32,
    ).reshape(ne, tok, hs)
    for g in range(2):
        sg_out[g] = sg_part[order[g]].astype(BF16)
    sg = send(sg_out, sg_in, {"expert": sib})
    rows_back(0)
    sg.wait_recv()
    sg_out2[...] = (sg_part[far] + sg_in[0].astype(F32)).astype(BF16)
    sg2 = send(sg_out2, sg_in2, {"expert": far})
    for s in range(half, nt):
        reduce_z(s)
    for i in range(1, here):
        rows_back(i)
    sg2.wait_recv()
    sgrad_ref[...] = (
        sg_part[e] + sg_in[1].astype(F32) + sg_in2[...].astype(F32)
    ).astype(BF16)
    total = jnp.zeros(next_ref.shape, F32)
    for s in range(nt):
        s3[s].wait_recv()
        total = total + s3_in[s].astype(F32)
    next_ref[...] = total.astype(BF16)
    for copy in copies:
        copy.wait_send()


def store_kernel(*refs):
    count = len(refs) // 2
    sems = refs[-1]
    moves = [
        pltpu.make_async_copy(refs[i], refs[count + i], sems.at[i]) for i in range(count)
    ]
    for move in moves:
        move.start()
    for move in moves:
        move.wait()


def fused(sizes, fr, fg, hidden, weight, shared, sweight, br, bg, cot):
    phases, ne, nt = sizes
    here, groups, cap, hq = hidden.shape[1:]
    tok, top = fr.shape[1:]
    features = weight.shape[3]
    dt = cot.shape[2]
    hs = shared.shape[2]
    vmem = pl.BlockSpec(memory_space=pltpu.VMEM)
    hbm = pl.BlockSpec(memory_space=pltpu.HBM)
    copies = 6 + (nt - 1) + 6 * nt + 2
    rows = ne * tok
    results = (
        jax.ShapeDtypeStruct((tok, dt), BF16),
        jax.ShapeDtypeStruct((here, cap, groups, hq), BF16),
        jax.ShapeDtypeStruct((tok, hs), BF16),
    )
    made = pl.pallas_call(
        functools.partial(fused_kernel, sizes),
        out_shape=results,
        in_specs=[hbm] * 9,
        out_specs=(vmem, vmem, vmem),
        scratch_shapes=[
            pltpu.VMEM((top, 1, tok), jnp.int32),
            pltpu.VMEM((top, 1, tok), F32),
            pltpu.VMEM((top, 1, tok), jnp.int32),
            pltpu.VMEM((top, 1, tok), F32),
            pltpu.VMEM((here, cap, groups, hq), BF16),
            pltpu.VMEM((here * hq, features), BF16),
            pltpu.VMEM((hs, dt), BF16),
            pltpu.VMEM((ne, tok, hs), BF16),
            pltpu.VMEM((nt, ne, tok, dt), BF16),
            pltpu.VMEM((ne, 2 * here * ne, 2 * tok), F32),
            pltpu.VMEM((rows, here * hq), BF16),
            pltpu.VMEM((rows, dt), F32),
            pltpu.VMEM((nt, 2, tok, dt), F32),
            pltpu.VMEM((nt, 2, tok, dt), BF16),
            pltpu.VMEM((nt, 2, tok, dt), BF16),
            pltpu.VMEM((nt, tok, dt), BF16),
            pltpu.VMEM((nt, tok, dt), BF16),
            pltpu.VMEM((nt, tok, dt), BF16),
            pltpu.VMEM((nt, tok, dt), BF16),
            pltpu.VMEM((rows, here * hq), F32),
            pltpu.VMEM((ne, tok, hs), F32),
            pltpu.VMEM((2, tok, hs), BF16),
            pltpu.VMEM((2, tok, hs), BF16),
            pltpu.VMEM((tok, hs), BF16),
            pltpu.VMEM((tok, hs), BF16),
            pltpu.SemaphoreType.DMA((copies,)),
            pltpu.SemaphoreType.DMA((copies,)),
            pltpu.SemaphoreType.DMA((9,)),
        ],
        compiler_params=pltpu.CompilerParams(
            collective_id=0, has_side_effects=True, vmem_limit_bytes=32 * 1024 * 1024
        ),
    )(
        *(
            pltpu.with_memory_space_constraint(a, pltpu.HBM)
            for a in (
                *(r.transpose(2, 0, 1) for r in (fr, fg, br, bg)),
                hidden[0].transpose(0, 2, 1, 3),
                weight.reshape(here * hq, features),
                shared[0], sweight[0], cot[0],
            )
        )
    )
    handed, hgrad, sgrad = pl.pallas_call(
        store_kernel,
        out_shape=results,
        in_specs=[vmem] * 3,
        out_specs=[hbm] * 3,
        scratch_shapes=[pltpu.SemaphoreType.DMA((3,))],
        compiler_params=pltpu.CompilerParams(vmem_limit_bytes=4 * 1024 * 1024),
    )(*made)
    return handed[None], hgrad.transpose(0, 2, 1, 3)[None], sgrad[None]


def shifted(value, axis, steps):
    count = lax.axis_size(axis)
    pairs = [(source, (source + steps) % count) for source in range(count)]
    return lax.ppermute(value, axis, pairs)


def slot_numbers(routes, experts):
    numbers = jnp.arange(experts, dtype=jnp.int32)
    onehot = (routes[:, :, None] == numbers[None, None, :]).astype(jnp.int32)
    per_token = jnp.sum(onehot, axis=1)
    before = jnp.cumsum(per_token, axis=0) - per_token
    return jnp.sum(onehot * before[:, None, :], axis=2)


def row_positions(routes, experts_here, groups, capacity):
    slot_index = slot_numbers(routes, experts_here * groups)
    holder = routes // experts_here
    within = routes - holder * experts_here
    return ((within * groups + holder) * capacity + slot_index).reshape(-1)


def place_rows(gates, values, positions, total_rows):
    scaled = (gates[:, :, None] * values[:, None, :].astype(jnp.float32)).astype(jnp.bfloat16)
    outgoing = jnp.zeros((total_rows, values.shape[1]), jnp.bfloat16)
    return outgoing.at[positions].set(scaled.reshape(-1, values.shape[1]))


def unfused(
    forward_routes,
    forward_gates,
    hidden_rows,
    down_weight,
    shared_hidden,
    shared_weight,
    backward_routes,
    backward_gates,
    cotangent,
):
    experts_here = down_weight.shape[1]
    features = down_weight.shape[3]
    capacity = hidden_rows.shape[3]
    groups = lax.axis_size("expert")
    token_count = forward_routes.shape[1]
    top_count = forward_routes.shape[2]
    hidden = hidden_rows[0]
    weight = down_weight[0]
    local_shared = shared_hidden[0]
    shared_piece = shared_weight[0]
    shared_part = jnp.dot(
        local_shared,
        lax.all_gather(shared_piece, "expert", axis=1, tiled=True),
        preferred_element_type=jnp.float32,
    )
    fore_positions = row_positions(forward_routes[0], experts_here, groups, capacity)
    fore_gates = forward_gates[0]
    partial_value = jnp.einsum(
        "egmh,ehd->egmd", hidden, weight, preferred_element_type=jnp.float32
    ).astype(jnp.bfloat16)
    arrived = lax.all_to_all(partial_value, "expert", split_axis=1, concat_axis=1, tiled=True)
    picked = arrived.reshape(-1, features)[fore_positions].reshape(token_count, top_count, features)
    summand = shared_part + jnp.sum(picked.astype(jnp.float32) * fore_gates[:, :, None], axis=1)
    summed = lax.psum_scatter(summand, "tensor", scatter_dimension=1, tiled=True)
    layer_out = summed.astype(jnp.bfloat16)
    handed = shifted(layer_out, "phase", 1)
    cotangent_whole = lax.all_gather(cotangent[0], "tensor", axis=1, tiled=True)
    back_positions = row_positions(backward_routes[0], experts_here, groups, capacity)
    total_rows = experts_here * groups * capacity
    outgoing = place_rows(backward_gates[0], cotangent_whole, back_positions, total_rows)
    received = lax.all_to_all(
        outgoing.reshape(experts_here, groups, capacity, features),
        "expert",
        split_axis=1,
        concat_axis=1,
        tiled=True,
    )
    hidden_back = jnp.einsum(
        "egmd,ehd->egmh", received, weight, preferred_element_type=jnp.float32
    ).astype(jnp.bfloat16)
    shared_back = lax.dot_general(
        cotangent_whole,
        lax.all_gather(shared_piece, "expert", axis=1, tiled=True),
        (((1,), (1,)), ((), ())),
        preferred_element_type=jnp.float32,
    )
    return (handed[None], hidden_back[None], shared_back.astype(jnp.bfloat16)[None])


def solution(mesh):
    sizes = tuple(mesh.shape[axis] for axis in ("phase", "expert", "tensor"))

    def on_device(*arrays):
        phases, ne, nt = sizes
        hidden, weight, cot = arrays[2], arrays[3], arrays[8]
        two_chips = ne == 4 and ne == nt and phases > 1
        fits = 2 * arrays[0].shape[1] <= LANES and cot.shape[2] % LANES == 0
        if two_chips and fits:
            return fused(sizes, *arrays)
        return unfused(*arrays)

    return jax.shard_map(
        on_device,
        mesh=mesh,
        in_specs=(
            P("phase", "expert", None),
            P("phase", "expert", None),
            P("phase", "expert", None, None, "tensor"),
            P("phase", "expert", "tensor", None),
            P("phase", "expert", "tensor"),
            P("phase", "tensor", "expert"),
            P("phase", "expert", None),
            P("phase", "expert", None),
            P("phase", "expert", "tensor"),
        ),
        out_specs=(
            P("phase", "expert", "tensor"),
            P("phase", "expert", None, None, "tensor"),
            P("phase", "expert", "tensor"),
        ),
        check_vma=False,
    )
```

```python
import functools

import jax
import jax.numpy as jnp
from jax import lax
from jax.experimental import pallas as pl
from jax.experimental.pallas import tpu as pltpu
from jax.sharding import PartitionSpec as P

MESH = pl.DeviceIdType.MESH
LANES = 128
F32 = jnp.float32
BF16 = jnp.bfloat16


def fused_kernel(
    sizes,
    fr_hbm, fg_hbm, br_hbm, bg_hbm,
    hid_hbm, w_hbm, sh_hbm, sw_hbm, cot_hbm,
    next_ref, hgrad_ref, sgrad_ref,
    fr, fg, br, bg,
    hid, w, sw, sh, cot, pack, hc, acc, keep,
    s1_out, s1_in, s2_out, s2_in, s3_out, s3_in,
    back, sg_part, sg_out, sg_in, sg_out2, sg_in2,
    send_sem, recv_sem, load_sem,
):
    phases, ne, nt = sizes
    ph, e, z = lax.axis_index("phase"), lax.axis_index("expert"), lax.axis_index("tensor")
    top, _, tok = fr.shape
    here, cap, _, hq = hid.shape
    dt = cot.shape[3]
    hs = sw.shape[0]
    experts = here * ne
    slots_all = cap * ne
    core = lax.rem(e, 2)
    sib = e + 1 - 2 * core
    far = lax.rem(e + 2, ne)
    far_sib = lax.rem(sib + 2, ne)
    others_t = [lax.rem(z + d, nt) for d in range(1, nt)]
    ahead, behind = lax.rem(ph + 1, phases), lax.rem(ph + phases - 1, phases)

    pairs = (
        (fr_hbm, fr), (fg_hbm, fg), (br_hbm, br), (bg_hbm, bg),
        (cot_hbm, cot.at[z, e]), (sh_hbm, sh.at[e]), (hid_hbm, hid), (w_hbm, w), (sw_hbm, sw),
    )
    loads = [pltpu.make_async_copy(a, b, load_sem.at[i]) for i, (a, b) in enumerate(pairs)]
    for load in loads:
        load.start()

    barrier = pltpu.get_barrier_semaphore()
    partners = [{"expert": sib}, {"expert": far}] + [{"tensor": o} for o in others_t]
    for step in range(nt):
        partners.append({"phase": ahead, "tensor": lax.rem(z + step, nt)})
        if phases > 2:
            partners.append({"phase": behind, "tensor": lax.rem(z + step, nt)})
    for partner in partners:
        pl.semaphore_signal(barrier, inc=1, device_id=partner, device_id_type=MESH)

    copies = []

    def send(src, dst, to):
        i = len(copies)
        copy = pltpu.make_async_remote_copy(
            src_ref=src, dst_ref=dst, send_sem=send_sem.at[i], recv_sem=recv_sem.at[i],
            device_id=to, device_id_type=MESH,
        )
        copy.start()
        copies.append(copy)
        return copy

    def spread(buffer):
        return [send(buffer.at[e], buffer.at[e], {"expert": o}) for o in (far, sib)]

    def hand_on(buffer, pair):
        pair[0].wait_recv()
        pair.append(send(buffer.at[far], buffer.at[far], {"expert": sib}))

    pl.semaphore_wait(barrier, len(partners))
    loads[4].wait()
    mine = cot.at[z, e]
    z_copies = [send(mine, mine, {"tensor": o}) for o in others_t]
    loads[5].wait()
    sh_copies = spread(sh)
    y_copies, sib_copies, far_copies = [], [], []

    for load in loads[:4]:
        load.wait()
    across = 2 * experts
    level = lax.broadcasted_iota(jnp.int32, (across, 2 * tok), 0)
    hot = jnp.zeros((across, 2 * tok), F32)
    gate = jnp.zeros((across, 2 * tok), F32)
    for k in range(top):
        named = jnp.concatenate([fr[k], br[k]], axis=1)
        weigh = jnp.concatenate([fg[k], bg[k]], axis=1)
        hot = jnp.where(named == level, 1.0, hot)
        gate = jnp.where(named + experts == level, weigh, gate)
    first = lax.broadcasted_iota(jnp.int32, (2 * tok, 2 * tok), 0)
    second = lax.broadcasted_iota(jnp.int32, (2 * tok, 2 * tok), 1)
    earlier = (first < second) & ((first < tok) == (second < tok))
    counts = jnp.dot(
        hot.astype(BF16), jnp.where(earlier, 1.0, 0.0).astype(BF16), preferred_element_type=F32
    )
    pack[e] = jnp.where(level < experts, jnp.where(hot > 0.5, counts, -1.0), gate)

    pack_copies = spread(pack)
    y_copies.append(send(mine, mine, {"expert": far}))
    sib_copies.append(send(mine, mine, {"expert": sib}))
    hand_on(sh, sh_copies)
    hand_on(pack, pack_copies)

    order = (far_sib, sib, far, e)
    level = lax.broadcasted_iota(jnp.int32, (tok, across), 1)
    entry = lax.broadcasted_iota(jnp.int32, (tok, slots_all), 1).astype(F32)

    def pick(table, at):
        return jnp.sum(jnp.where(level == at, table, 0.0), axis=1, keepdims=True)

    pack_copies[1].wait_recv()
    pack_copies[2].wait_recv()
    loads[6].wait()
    hidden = [hid[i].reshape(slots_all, hq) for i in range(here)]
    for n, b in enumerate(order):
        table = pack[b].T[:tok]
        offset = b.astype(F32)
        for i in range(here):
            x = e * here + i
            place = jnp.where(pick(table, x) * ne + offset == entry, 1.0, 0.0).astype(BF16)
            rows = jnp.dot(place, hidden[i], preferred_element_type=F32)
            hc[n * tok:(n + 1) * tok, i * hq:(i + 1) * hq] = (
                rows * pick(table, experts + x)
            ).astype(BF16)

    def relay(d):
        z_copies[d - 1].wait_recv()
        piece = cot.at[lax.rem(z + nt - d, nt), e]
        y_copies.append(send(piece, piece, {"expert": far}))
        sib_copies.append(send(piece, piece, {"expert": sib}))

    def hand_over(d):
        y_copies[d].wait_recv()
        piece = cot.at[lax.rem(z + nt - d, nt), far]
        far_copies.append(send(piece, piece, {"expert": sib}))

    relay(1)
    hand_over(0)
    loads[7].wait()
    loads[8].wait()
    sh_copies[1].wait_recv()
    sh_copies[2].wait_recv()
    s1, s2, s3 = [], [], []
    for s in range(nt):
        f = lax.rem(z + 1 + s, nt)
        cols = pl.ds(pl.multiple_of(f * dt, LANES), dt)
        acc[...] = jnp.dot(hc[...], w[:, cols], preferred_element_type=F32)

        @pl.when(f == e)
        def _():
            shared = jnp.concatenate([sh[b] for b in order], axis=0)
            acc[...] += jnp.dot(shared, sw[...], preferred_element_type=F32)

        for g in range(2):
            s1_out[s, g] = acc[g * tok:(g + 1) * tok, :].astype(BF16)
        s1.append(send(s1_out.at[s], s1_in.at[s], {"expert": sib}))
        for g in range(2):
            keep[s, g] = acc[(2 + g) * tok:(3 + g) * tok, :]

    def reduce_core(s):
        s1[s].wait_recv()
        s2_out[s] = (keep[s, 0] + s1_in[s, 0].astype(F32)).astype(BF16)
        s2.append(send(s2_out.at[s], s2_in.at[s], {"expert": far}))
        keep[s, 1] = keep[s, 1] + s1_in[s, 1].astype(F32)

    def back_part(d):
        f = lax.rem(z + nt - d, nt)
        sib_copies[d].wait_recv()
        far_copies[d].wait_recv()
        cols = pl.ds(pl.multiple_of(f * dt, LANES), dt)
        part = lax.dot_general(
            cot[f].reshape(ne * tok, dt), w[:, cols], (((1,), (1,)), ((), ())),
            preferred_element_type=F32,
        )
        if d == 0:
            back[...] = part
        else:
            back[...] += part

    def reduce_z(s):
        s2[s].wait_recv()
        s3_out[s] = (keep[s, 1] + s2_in[s].astype(F32)).astype(BF16)
        to = {"phase": ahead, "tensor": others_t[s] if s < nt - 1 else z}
        s3.append(send(s3_out.at[s], s3_in.at[s], to))

    def rows_back(i):
        x = e * here + i
        at = [pack[b, pl.ds(x, 1), :][:, tok:] for b in range(ne)]
        named = jnp.concatenate([a * ne + b for b, a in enumerate(at)], axis=1)
        entry_down = lax.broadcasted_iota(jnp.int32, (slots_all, ne * tok), 0).astype(F32)
        place = jnp.where(named == entry_down, 1.0, 0.0).astype(BF16)
        gates = jnp.concatenate([pick(pack[b].T[tok:], experts + x) for b in range(ne)], axis=0)
        rows = (back[:, i * hq:(i + 1) * hq] * gates).astype(BF16)
        hgrad_ref[i] = jnp.dot(place, rows, preferred_element_type=F32).astype(BF16).reshape(
            cap, ne, hq
        )

    half = nt // 2
    for d in range(2, nt - 1):
        relay(d)
    for s in range(half):
        reduce_core(s)
    relay(nt - 1)
    for d in range(1, half):
        hand_over(d)
    for s in range(half, nt):
        reduce_core(s)
    for d in range(half):
        back_part(d)
    for s in range(half):
        reduce_z(s)
    for d in range(half, nt):
        hand_over(d)
    for d in range(half, nt):
        back_part(d)

    sg_part[...] = lax.dot_general(
        cot[e].reshape(ne * tok, dt), sw[...], (((1,), (1,)), ((), ())),
        preferred_element_type=F32,
    ).reshape(ne, tok, hs)
    for g in range(2):
        sg_out[g] = sg_part[order[g]].astype(BF16)
    sg = send(sg_out, sg_in, {"expert": sib})
    rows_back(0)
    sg.wait_recv()
    sg_out2[...] = (sg_part[far] + sg_in[0].astype(F32)).astype(BF16)
    sg2 = send(sg_out2, sg_in2, {"expert": far})
    for s in range(half, nt):
        reduce_z(s)
    for i in range(1, here):
        rows_back(i)
    sg2.wait_recv()
    sgrad_ref[...] = (
        sg_part[e] + sg_in[1].astype(F32) + sg_in2[...].astype(F32)
    ).astype(BF16)
    total = jnp.zeros(next_ref.shape, F32)
    for s in range(nt):
        s3[s].wait_recv()
        total = total + s3_in[s].astype(F32)
    next_ref[...] = total.astype(BF16)
    for copy in copies:
        copy.wait_send()


def store_kernel(*refs):
    count = len(refs) // 2
    sems = refs[-1]
    moves = [
        pltpu.make_async_copy(refs[i], refs[count + i], sems.at[i]) for i in range(count)
    ]
    for move in moves:
        move.start()
    for move in moves:
        move.wait()


def fused(sizes, fr, fg, hidden, weight, shared, sweight, br, bg, cot):
    phases, ne, nt = sizes
    here, groups, cap, hq = hidden.shape[1:]
    tok, top = fr.shape[1:]
    features = weight.shape[3]
    dt = cot.shape[2]
    hs = shared.shape[2]
    vmem = pl.BlockSpec(memory_space=pltpu.VMEM)
    hbm = pl.BlockSpec(memory_space=pltpu.HBM)
    copies = 6 + (nt - 1) + 6 * nt + 2
    rows = ne * tok
    results = (
        jax.ShapeDtypeStruct((tok, dt), BF16),
        jax.ShapeDtypeStruct((here, cap, groups, hq), BF16),
        jax.ShapeDtypeStruct((tok, hs), BF16),
    )
    made = pl.pallas_call(
        functools.partial(fused_kernel, sizes),
        out_shape=results,
        in_specs=[hbm] * 9,
        out_specs=(vmem, vmem, vmem),
        scratch_shapes=[
            pltpu.VMEM((top, 1, tok), jnp.int32),
            pltpu.VMEM((top, 1, tok), F32),
            pltpu.VMEM((top, 1, tok), jnp.int32),
            pltpu.VMEM((top, 1, tok), F32),
            pltpu.VMEM((here, cap, groups, hq), BF16),
            pltpu.VMEM((here * hq, features), BF16),
            pltpu.VMEM((hs, dt), BF16),
            pltpu.VMEM((ne, tok, hs), BF16),
            pltpu.VMEM((nt, ne, tok, dt), BF16),
            pltpu.VMEM((ne, 2 * here * ne, 2 * tok), F32),
            pltpu.VMEM((rows, here * hq), BF16),
            pltpu.VMEM((rows, dt), F32),
            pltpu.VMEM((nt, 2, tok, dt), F32),
            pltpu.VMEM((nt, 2, tok, dt), BF16),
            pltpu.VMEM((nt, 2, tok, dt), BF16),
            pltpu.VMEM((nt, tok, dt), BF16),
            pltpu.VMEM((nt, tok, dt), BF16),
            pltpu.VMEM((nt, tok, dt), BF16),
            pltpu.VMEM((nt, tok, dt), BF16),
            pltpu.VMEM((rows, here * hq), F32),
            pltpu.VMEM((ne, tok, hs), F32),
            pltpu.VMEM((2, tok, hs), BF16),
            pltpu.VMEM((2, tok, hs), BF16),
            pltpu.VMEM((tok, hs), BF16),
            pltpu.VMEM((tok, hs), BF16),
            pltpu.SemaphoreType.DMA((copies,)),
            pltpu.SemaphoreType.DMA((copies,)),
            pltpu.SemaphoreType.DMA((9,)),
        ],
        compiler_params=pltpu.CompilerParams(
            collective_id=0, has_side_effects=True, vmem_limit_bytes=32 * 1024 * 1024
        ),
    )(
        *(
            pltpu.with_memory_space_constraint(a, pltpu.HBM)
            for a in (
                *(r.transpose(2, 0, 1) for r in (fr, fg, br, bg)),
                hidden[0].transpose(0, 2, 1, 3),
                weight.reshape(here * hq, features),
                shared[0], sweight[0], cot[0],
            )
        )
    )
    handed, hgrad, sgrad = pl.pallas_call(
        store_kernel,
        out_shape=results,
        in_specs=[vmem] * 3,
        out_specs=[hbm] * 3,
        scratch_shapes=[pltpu.SemaphoreType.DMA((3,))],
        compiler_params=pltpu.CompilerParams(vmem_limit_bytes=4 * 1024 * 1024),
    )(*made)
    return handed[None], hgrad.transpose(0, 2, 1, 3)[None], sgrad[None]


def shifted(value, axis, steps):
    count = lax.axis_size(axis)
    pairs = [(source, (source + steps) % count) for source in range(count)]
    return lax.ppermute(value, axis, pairs)


def slot_numbers(routes, experts):
    numbers = jnp.arange(experts, dtype=jnp.int32)
    onehot = (routes[:, :, None] == numbers[None, None, :]).astype(jnp.int32)
    per_token = jnp.sum(onehot, axis=1)
    before = jnp.cumsum(per_token, axis=0) - per_token
    return jnp.sum(onehot * before[:, None, :], axis=2)


def row_positions(routes, experts_here, groups, capacity):
    slot_index = slot_numbers(routes, experts_here * groups)
    holder = routes // experts_here
    within = routes - holder * experts_here
    return ((within * groups + holder) * capacity + slot_index).reshape(-1)


def place_rows(gates, values, positions, total_rows):
    scaled = (gates[:, :, None] * values[:, None, :].astype(jnp.float32)).astype(jnp.bfloat16)
    outgoing = jnp.zeros((total_rows, values.shape[1]), jnp.bfloat16)
    return outgoing.at[positions].set(scaled.reshape(-1, values.shape[1]))


def unfused(
    forward_routes,
    forward_gates,
    hidden_rows,
    down_weight,
    shared_hidden,
    shared_weight,
    backward_routes,
    backward_gates,
    cotangent,
):
    experts_here = down_weight.shape[1]
    features = down_weight.shape[3]
    capacity = hidden_rows.shape[3]
    groups = lax.axis_size("expert")
    token_count = forward_routes.shape[1]
    top_count = forward_routes.shape[2]
    hidden = hidden_rows[0]
    weight = down_weight[0]
    local_shared = shared_hidden[0]
    shared_piece = shared_weight[0]
    shared_part = jnp.dot(
        local_shared,
        lax.all_gather(shared_piece, "expert", axis=1, tiled=True),
        preferred_element_type=jnp.float32,
    )
    fore_positions = row_positions(forward_routes[0], experts_here, groups, capacity)
    fore_gates = forward_gates[0]
    partial_value = jnp.einsum(
        "egmh,ehd->egmd", hidden, weight, preferred_element_type=jnp.float32
    ).astype(jnp.bfloat16)
    arrived = lax.all_to_all(partial_value, "expert", split_axis=1, concat_axis=1, tiled=True)
    picked = arrived.reshape(-1, features)[fore_positions].reshape(token_count, top_count, features)
    summand = shared_part + jnp.sum(picked.astype(jnp.float32) * fore_gates[:, :, None], axis=1)
    summed = lax.psum_scatter(summand, "tensor", scatter_dimension=1, tiled=True)
    layer_out = summed.astype(jnp.bfloat16)
    handed = shifted(layer_out, "phase", 1)
    cotangent_whole = lax.all_gather(cotangent[0], "tensor", axis=1, tiled=True)
    back_positions = row_positions(backward_routes[0], experts_here, groups, capacity)
    total_rows = experts_here * groups * capacity
    outgoing = place_rows(backward_gates[0], cotangent_whole, back_positions, total_rows)
    received = lax.all_to_all(
        outgoing.reshape(experts_here, groups, capacity, features),
        "expert",
        split_axis=1,
        concat_axis=1,
        tiled=True,
    )
    hidden_back = jnp.einsum(
        "egmd,ehd->egmh", received, weight, preferred_element_type=jnp.float32
    ).astype(jnp.bfloat16)
    shared_back = lax.dot_general(
        cotangent_whole,
        lax.all_gather(shared_piece, "expert", axis=1, tiled=True),
        (((1,), (1,)), ((), ())),
        preferred_element_type=jnp.float32,
    )
    return (handed[None], hidden_back[None], shared_back.astype(jnp.bfloat16)[None])


def solution(mesh):
    sizes = tuple(mesh.shape[axis] for axis in ("phase", "expert", "tensor"))

    def on_device(*arrays):
        phases, ne, nt = sizes
        hidden, weight, cot = arrays[2], arrays[3], arrays[8]
        two_chips = ne == 4 and ne == nt and phases > 1
        fits = 2 * arrays[0].shape[1] <= LANES and cot.shape[2] % LANES == 0
        if two_chips and fits:
            return fused(sizes, *arrays)
        return unfused(*arrays)

    return jax.shard_map(
        on_device,
        mesh=mesh,
        in_specs=(
            P("phase", "expert", None),
            P("phase", "expert", None),
            P("phase", "expert", None, None, "tensor"),
            P("phase", "expert", "tensor", None),
            P("phase", "expert", "tensor"),
            P("phase", "tensor", "expert"),
            P("phase", "expert", None),
            P("phase", "expert", None),
            P("phase", "expert", "tensor"),
        ),
        out_specs=(
            P("phase", "expert", "tensor"),
            P("phase", "expert", None, None, "tensor"),
            P("phase", "expert", "tensor"),
        ),
        check_vma=False,
    )
```
